32 devices in a mesh: img: 4 (over x, core), tok: 8 (over z, y).
Axes of the slice: x: 2, y: 2, z: 4, core: 2. Of those that a mesh axis runs over, the one named last changes fastest.
Arguments:
- student: bfloat16 [4, 1024, 4096], P('img', None, 'tok'), may hold values from -0.32 to 0.32
- teacher: bfloat16 [4, 64, 64, 4096], P('img', None, None, 'tok'), may hold values from -160 to 160
Outputs:
- gradient: bfloat16 [4, 1024, 4096], P('img', None, 'tok')
- loss: float32 [], replicated
The draws below stay inside these ranges and needn't reach their ends.
All inputs are finite; a program needn't handle non-finite values.
Results may differ from the reference program's by a relative error of at most 0.0069.
Values may be sent and summed in bfloat16 or wider, within the bound.
A program may use at most 64 MiB of HBM per device.

```python
import math
import jax
import jax.numpy as jnp
from jax import lax

D = 4096
GH = 32
GW = 32
HRH = 64
HRW = 64
P_SIZE = 1024
IMAGES = 4


def feature_values(key, shape, width, base_scale):
    first = jax.random.fold_in(key, 0)
    position = jnp.arange(width, dtype=jnp.float32) / max(width - 1, 1)
    ramp = jnp.exp(position * math.log(3.0))
    noise = jnp.clip(jax.random.normal(first, shape, jnp.float32), -4.0, 4.0)
    return base_scale * noise * ramp


def draw_student(key, part):
    values = feature_values(jax.random.fold_in(key, 11), (IMAGES, P_SIZE, D), D, 0.002)
    return values.astype(jnp.bfloat16)


def draw_teacher(key, part):
    values = feature_values(jax.random.fold_in(key, 23), (IMAGES, HRH, HRW, D), D, 1.0)
    return values.astype(jnp.bfloat16)


def setup_inputs(seed: int = 0) -> dict:
    keys = jax.random.split(jax.random.key(seed), 3)
    return {
        "student": draw_student(jax.random.fold_in(keys[2], 71), 0),
        "teacher": draw_teacher(jax.random.fold_in(keys[2], 71), 0),
    }


cubic_taps = (-0.09375, 0.59375, 0.59375, -0.09375)
epsilon = 1e-06

def shrink(padded, length, dimension):
    weighted = [cubic_taps[offset] * lax.slice_in_dim(padded, offset, offset + 2 * length - 1, 2, dimension).astype(jnp.float32) for offset in range(4)]
    return weighted[0] + weighted[1] + weighted[2] + weighted[3]

def one_image(inputs):
    student_rows, teacher_grid = inputs
    padded = jnp.pad(teacher_grid, ((1, 1), (1, 1), (0, 0)), mode='edge')
    vertical = shrink(padded, GH, 0)
    shrunk = shrink(vertical, GW, 1).reshape(P_SIZE, D)
    teacher_unit = (shrunk * lax.rsqrt(lax.optimization_barrier(jnp.sum(shrunk * shrunk, axis=1, keepdims=True)) + epsilon)).astype(jnp.bfloat16)
    features = student_rows.astype(jnp.float32)
    inverse = lax.rsqrt(lax.optimization_barrier(jnp.sum(features * features, axis=1, keepdims=True)) + epsilon)
    unit_rows = features * inverse
    unit_low = unit_rows.astype(jnp.bfloat16)
    mismatch = jnp.dot(unit_low, unit_low.T, preferred_element_type=jnp.float32) - jnp.dot(teacher_unit, teacher_unit.T, preferred_element_type=jnp.float32)
    squared = jnp.sum(mismatch * mismatch)
    pull_grad = 4.0 * jnp.dot(mismatch.astype(jnp.bfloat16), unit_low, preferred_element_type=jnp.float32)
    gradient = inverse * pull_grad - inverse * unit_rows * lax.optimization_barrier(jnp.sum(unit_rows * pull_grad, axis=1, keepdims=True))
    return (gradient.astype(jnp.bfloat16), squared)

def reference(student, teacher):
    gradients, losses = lax.map(one_image, (student, teacher))
    return (gradients, jnp.sum(losses) / P_SIZE)
```

```python
import functools

import jax
import jax.numpy as jnp
from jax import lax
from jax.experimental import pallas as pl
from jax.experimental.pallas import tpu as pltpu
from jax.sharding import PartitionSpec as P

cubic_taps = (-0.09375, 0.59375, 0.59375, -0.09375)
epsilon = 1e-06
LANES = 128
BLOCK = 256
SPLIT = 2
LAG = 2
CHUNKS = 4
UNROLL = 2


def lane_tiles_sum(x):
    total = x[:, :LANES]
    for start in range(LANES, x.shape[1], LANES):
        total = total + x[:, start : start + LANES]
    return total


def spread(column, width):
    return jnp.concatenate([column] * (width // LANES), axis=1)


def kernel(
    sizes, student_hbm, teacher_hbm, out_ref, loss_ref,
    sbuf, tbuf, vbuf, shrunk, unit_low, teach_low, part, tpart, inv, tinv,
    norms, along, losses, img_losses,
    own, prefix, theirs, ysend, yrecv, zin, zout, mlow, pull, sqacc,
    load_sem, s_send, s_recv, a_send, a_recv, l_send, l_recv,
    i_send, i_recv, y_send, y_recv, z_send, z_recv, g_send, g_recv,
):
    n, m = sizes
    tokens, feats = unit_low.shape
    height, width = tbuf.shape[0] - 2, tbuf.shape[1]
    half_w = width // 2
    lane_tiles = feats // LANES
    nb = tokens // BLOCK
    tiles = tokens // LANES
    me = lax.axis_index("tok")
    img = lax.axis_index("img")
    col = lax.rem(me, 2)
    row = me // 2
    chain = n // 2
    square = [(i, i) for i in range(nb)]
    upper = [(i, j) for i in range(nb) for j in range(i + 1, nb)]
    diag, off = len(square) // 2, len(upper) // 2
    pairs = upper[:off] + square[:diag] + upper[off:] + square[diag:]
    half = diag + off
    count = half * SPLIT
    depth = BLOCK // SPLIT
    early = jnp.where(row < (chain + 1) // 2, 0, 1)
    late = 1 - early
    rank = jnp.minimum(row, chain - 1 - row)

    student_load = pltpu.make_async_copy(student_hbm.at[0], sbuf, load_sem.at[0])
    student_load.start()

    def load(index, first, last, to):
        copy = pltpu.make_async_copy(
            teacher_hbm.at[0, first:last],
            tbuf.at[to : to + last - first],
            load_sem.at[index],
        )
        copy.start()
        return copy

    step = height // CHUNKS
    top = load(1, 0, 1, 0)
    loads = []
    for q in range(CHUNKS):
        first = q * step + 1 if q else 0
        last = height if q == CHUNKS - 1 else (q + 1) * step + 1
        loads.append(load(3 + q, first, last, first + 1))
    bottom = load(2, height - 1, height, height + 1)

    barrier = pltpu.get_barrier_semaphore()
    for p in range(1, n):
        pl.semaphore_signal(barrier, 1, device_id={"tok": lax.rem(me + p, n)})
    for p in range(1, m):
        pl.semaphore_signal(barrier, 1, device_id={"img": lax.rem(img + p, m)})

    def gather_copies(buf, send, recv, axis, here, size):
        return [
            pltpu.make_async_remote_copy(
                src_ref=buf.at[here],
                dst_ref=buf.at[here],
                send_sem=send.at[p - 1],
                recv_sem=recv.at[p - 1],
                device_id={axis: lax.rem(here + p, size)},
            )
            for p in range(1, size)
        ]

    def pack_rows(sources):
        lane = lax.broadcasted_iota(jnp.int32, (LANES, LANES), 1)
        columns = jnp.zeros((LANES, LANES), jnp.float32)
        for k, source in enumerate(sources):
            for b in range(tiles):
                block = source[b * LANES : (b + 1) * LANES, :]
                total = jnp.sum(block, axis=1, keepdims=True)
                columns = jnp.where(lane == k * tiles + b, total, columns)
        return columns.T[: len(sources) * tiles]

    def summed(buf, size):
        total = buf[0]
        for k in range(1, size):
            total = total + buf[k]
        return total

    def unpack_rows(values, targets):
        blank = jnp.zeros((LANES - values.shape[0], LANES), jnp.float32)
        columns = jnp.concatenate([values, blank], axis=0).T
        for k, target in enumerate(targets):
            for b in range(tiles):
                at = k * tiles + b
                target[b * LANES : (b + 1) * LANES, :] = jnp.broadcast_to(
                    columns[:, at : at + 1], (LANES, LANES)
                )

    def slab(b):
        return pl.ds(pl.multiple_of(b * LANES, LANES), LANES)

    @pl.when(rank == 0)
    def _():
        zin[early] = jnp.zeros(zin.shape[1:], zin.dtype)

    sqacc[...] = jnp.zeros_like(sqacc)
    student_load.wait()

    @pl.loop(0, tiles)
    def _(b):
        x = sbuf[slab(b), :].astype(jnp.float32)
        part[slab(b), :] = lane_tiles_sum(x * x)

    def shrink_pair(first):
        for u in range(UNROLL):
            a = first * UNROLL + u
            x = [tbuf[2 * a + k].astype(jnp.float32) for k in range(4)]
            v = cubic_taps[1] * (x[1] + x[2]) + cubic_taps[0] * (x[0] + x[3])
            for t in range(lane_tiles):
                tile = v[:, t * LANES : (t + 1) * LANES]
                vbuf[u, t, 8 : 8 + width, :] = tile
                vbuf[u, t, 7:8, :] = tile[0:1]
                vbuf[u, t, 8 + width : 9 + width, :] = tile[width - 1 : width]
        for u in range(UNROLL):
            a = first * UNROLL + u
            rows = pl.ds(pl.multiple_of(a * half_w, half_w), half_w)
            total = None
            for t in range(lane_tiles):
                w = [vbuf[u, t, pl.ds(7 + k, half_w, stride=2), :] for k in range(4)]
                h = cubic_taps[1] * (w[1] + w[2]) + cubic_taps[0] * (w[0] + w[3])
                shrunk[rows, t * LANES : (t + 1) * LANES] = h
                total = h * h if total is None else total + h * h
            tpart[rows, :] = total

    top.wait()
    for q in range(CHUNKS):
        loads[q].wait()
        if q == CHUNKS - 1:
            bottom.wait()
        trips = step // 2 // UNROLL
        pl.loop(q * trips, (q + 1) * trips)(shrink_pair)

    norms[me] = pack_rows((part, tpart))
    pl.semaphore_wait(barrier, n - 1 + m - 1)
    s_copies = gather_copies(norms, s_send, s_recv, "tok", me, n)
    for copy in s_copies:
        copy.start()
    for copy in s_copies:
        copy.wait_recv()
    unpack_rows(lax.rsqrt(summed(norms, n) + epsilon), (inv, tinv))

    @pl.loop(0, tiles)
    def _(b):
        x = sbuf[slab(b), :].astype(jnp.float32) * spread(inv[slab(b), :], feats)
        unit_low[slab(b), :] = x.astype(jnp.bfloat16)

    def pick(k, c):
        first, second = pairs[k], pairs[half + k]
        i = first[0] + c * (second[0] - first[0])
        j = first[1] + c * (second[1] - first[1])
        return i, j

    def strip(i):
        return pl.ds(pl.multiple_of(i * BLOCK, BLOCK), BLOCK)

    def gram(low, i, j):
        return lax.dot_general(
            low[strip(i), :], low[strip(j), :], (((1,), (1,)), ((), ())),
            preferred_element_type=jnp.float32,
        )

    for k in range(half):
        theirs[k] = gram(unit_low, *pick(k, 1 - col))
    for k in range(half):
        pieces = gram(unit_low, *pick(k, col))
        own[k * SPLIT : (k + 1) * SPLIT] = pieces.reshape(SPLIT, depth, BLOCK)

    @pl.loop(0, tiles)
    def _(b):
        x = shrunk[slab(b), :] * spread(tinv[slab(b), :], feats)
        teach_low[slab(b), :] = x.astype(jnp.bfloat16)

    def skip(k):
        return (k % SPLIT) * depth if k >= off * SPLIT else 0

    y_copies = []
    for k in range(half):
        d = theirs[k] - gram(teach_low, *pick(k, 1 - col))
        pieces = d.astype(jnp.bfloat16).reshape(SPLIT, depth, BLOCK)
        ysend[k * SPLIT : (k + 1) * SPLIT] = pieces
        for t in range(k * SPLIT, (k + 1) * SPLIT):
            copy = pltpu.make_async_remote_copy(
                src_ref=ysend.at[t, :, skip(t) :], dst_ref=yrecv.at[t, :, skip(t) :],
                send_sem=y_send.at[t], recv_sem=y_recv.at[t],
                device_id={"tok": me + 1 - 2 * col},
            )
            copy.start()
            y_copies.append(copy)
    for k in range(half):
        d = gram(teach_low, *pick(k, col)).reshape(SPLIT, depth, BLOCK)
        own[k * SPLIT : (k + 1) * SPLIT] = own[k * SPLIT : (k + 1) * SPLIT] - d

    def chain_copy(direction, k):
        step = 2 - 4 * direction
        return pltpu.make_async_remote_copy(
            src_ref=zout.at[direction, k, :, skip(k) :],
            dst_ref=zin.at[direction, k, :, skip(k) :],
            send_sem=z_send.at[direction, k], recv_sem=z_recv.at[direction, k],
            device_id={"tok": lax.rem(me + step + n, n)},
        )

    def piece(k, c):
        i, j = pick(k // SPLIT, c)
        start = i * BLOCK + (k % SPLIT) * depth
        columns = pl.ds(pl.multiple_of(j * BLOCK + skip(k), depth), BLOCK - skip(k))
        return i, j, pl.ds(pl.multiple_of(start, depth), depth), columns

    def mirror(k, c, block):
        _, j, rows, _ = piece(k, c)
        first = 0
        if k >= off * SPLIT:
            first = skip(k) + depth
            block = block[:, depth:]
        if first < BLOCK:
            start = pl.multiple_of(j * BLOCK + first, depth)
            mlow[pl.ds(start, BLOCK - first), rows] = block.T.astype(jnp.bfloat16)

    def block_copy(k):
        _, _, rows, columns = piece(k, col)
        block = mlow.at[rows, columns]
        return pltpu.make_async_remote_copy(
            src_ref=block, dst_ref=block,
            send_sem=g_send.at[k], recv_sem=g_recv.at[k],
            device_id={"tok": me + 1 - 2 * col},
        )

    def run_early(k):
        y_copies[k].wait_recv()
        cut = skip(k)
        mine = own[k, :, cut:] + yrecv[k, :, cut:].astype(jnp.float32)
        copy = chain_copy(early, k)

        @pl.when(rank > 0)
        def _():
            copy.wait_recv()

        total = mine + zin[early, k, :, cut:].astype(jnp.float32)
        zout[early, k, :, cut:] = total.astype(jnp.bfloat16)
        own[k, :, cut:] = mine
        prefix[k, :, cut:] = total
        copy.start()

    def run_late(k):
        copy = chain_copy(late, k)
        copy.wait_recv()
        cut = skip(k)
        incoming = zin[late, k, :, cut:].astype(jnp.float32)
        total = prefix[k, :, cut:] + incoming
        _, _, rows, columns = piece(k, col)
        low = total.astype(jnp.bfloat16)

        @pl.when(rank > 0)
        def _():
            zout[late, k, :, cut:] = (own[k, :, cut:] + incoming).astype(jnp.bfloat16)
            copy.start()

        mlow[rows, columns] = low
        block_copy(k).start()
        sums = jnp.sum(total * total, axis=0, keepdims=True)
        if k >= off * SPLIT:
            sqacc[:, :depth] += sums[:, :depth]
            if cut + depth < BLOCK:
                sqacc[:, cut + depth :] += 2.0 * sums[:, depth:]
        else:
            sqacc[...] += 2.0 * sums
        mirror(k, col, total)

    def run_chain(lag):
        for t in range(count + lag):
            if t < count:
                run_early(t)
            if t >= lag:
                run_late(t - lag)

    @pl.when(rank == 0)
    def _():
        run_chain(count)

    @pl.when(rank > 0)
    def _():
        run_chain(min(LAG, count))

    squared = jnp.sum(sqacc[...], axis=1, keepdims=True)
    losses[me] = jnp.broadcast_to(squared, losses.shape[1:])
    l_copies = gather_copies(losses, l_send, l_recv, "tok", me, n)
    for copy in l_copies:
        copy.start()

    for k in range(count):
        block_copy(k).wait_recv()
        _, _, rows, columns = piece(k, 1 - col)
        mirror(k, 1 - col, mlow[rows, columns].astype(jnp.float32))

    @pl.loop(0, nb)
    def _(b):
        rows = strip(b)
        p = 4.0 * jnp.dot(mlow[rows, :], unit_low[...], preferred_element_type=jnp.float32)
        pull[rows, :] = p
        unit = sbuf[rows, :].astype(jnp.float32) * spread(inv[rows, :], feats)
        part[rows, :] = lane_tiles_sum(unit * p)

    along[me] = pack_rows((part,))
    a_copies = gather_copies(along, a_send, a_recv, "tok", me, n)
    for copy in a_copies:
        copy.start()

    for copy in l_copies:
        copy.wait_recv()
    img_losses[img] = summed(losses, n)
    i_copies = gather_copies(img_losses, i_send, i_recv, "img", img, m)
    for copy in i_copies:
        copy.start()

    for copy in a_copies:
        copy.wait_recv()
    unpack_rows(summed(along, n), (tinv,))

    @pl.loop(0, tiles)
    def _(b):
        scale = spread(inv[slab(b), :], feats)
        unit = sbuf[slab(b), :].astype(jnp.float32) * scale
        grad = scale * pull[slab(b), :] - scale * unit * spread(tinv[slab(b), :], feats)
        out_ref[0, slab(b), :] = grad.astype(out_ref.dtype)

    for copy in i_copies:
        copy.wait_recv()
    loss_ref[...] = summed(img_losses, m) / (chain * tokens)

    for copy in s_copies + l_copies + a_copies + i_copies + y_copies:
        copy.wait_send()
    for k in range(count):
        block_copy(k).wait_send()
        chain_copy(early, k).wait_send()

        @pl.when(rank > 0)
        def _():
            chain_copy(late, k).wait_send()


def per_device(n, m, student, teacher):
    _, tokens, feats = student.shape
    _, height, width, _ = teacher.shape
    nb = tokens // BLOCK
    half = nb // 2 + nb * (nb - 1) // 4
    count = half * SPLIT
    depth = BLOCK // SPLIT
    tiles = tokens // LANES
    f32, bf16 = jnp.float32, jnp.bfloat16
    vmem, dma = pltpu.VMEM, pltpu.SemaphoreType.DMA
    gradient, loss = pl.pallas_call(
        functools.partial(kernel, (n, m)),
        name="anchor",
        out_shape=(
            jax.ShapeDtypeStruct(student.shape, bf16),
            jax.ShapeDtypeStruct((8, LANES), f32),
        ),
        in_specs=[
            pl.BlockSpec(memory_space=pl.ANY),
            pl.BlockSpec(memory_space=pl.ANY),
        ],
        out_specs=(
            pl.BlockSpec(memory_space=pltpu.VMEM),
            pl.BlockSpec(memory_space=pltpu.VMEM),
        ),
        scratch_shapes=[
            vmem((tokens, feats), bf16),
            vmem((height + 2, width, feats), bf16),
            vmem((UNROLL, feats // LANES, width + 16, LANES), f32),
            vmem((tokens, feats), f32),
            vmem((tokens, feats), bf16),
            vmem((tokens, feats), bf16),
            vmem((tokens, LANES), f32),
            vmem((tokens, LANES), f32),
            vmem((tokens, LANES), f32),
            vmem((tokens, LANES), f32),
            vmem((n, 2 * tiles, LANES), f32),
            vmem((n, tiles, LANES), f32),
            vmem((n, 8, LANES), f32),
            vmem((m, 8, LANES), f32),
            vmem((count, depth, BLOCK), f32),
            vmem((count, depth, BLOCK), f32),
            vmem((half, BLOCK, BLOCK), f32),
            vmem((count, depth, BLOCK), bf16),
            vmem((count, depth, BLOCK), bf16),
            vmem((2, count, depth, BLOCK), bf16),
            vmem((2, count, depth, BLOCK), bf16),
            vmem((tokens, tokens), bf16),
            vmem((tokens, feats), f32),
            vmem((1, BLOCK), f32),
            dma((CHUNKS + 3,)),
            dma((n - 1,)), dma((n - 1,)),
            dma((n - 1,)), dma((n - 1,)), dma((n - 1,)), dma((n - 1,)),
            dma((m - 1,)), dma((m - 1,)),
            dma((count,)), dma((count,)),
            dma((2, count)), dma((2, count)),
            dma((count,)), dma((count,)),
        ],
        compiler_params=pltpu.CompilerParams(
            collective_id=0, has_side_effects=True, vmem_limit_bytes=56 * 1024 * 1024
        ),
    )(student, teacher)
    return gradient, loss[0, 0]


def solution(mesh):
    return jax.shard_map(
        functools.partial(per_device, mesh.shape["tok"], mesh.shape["img"]),
        mesh=mesh,
        in_specs=(P("img", None, "tok"), P("img", None, None, "tok")),
        out_specs=(P("img", None, "tok"), P()),
        check_vma=False,
    )
```

```python
import functools

import jax
import jax.numpy as jnp
from jax import lax
from jax.experimental import pallas as pl
from jax.experimental.pallas import tpu as pltpu
from jax.sharding import PartitionSpec as P

cubic_taps = (-0.09375, 0.59375, 0.59375, -0.09375)
epsilon = 1e-06
LANES = 128
BLOCK = 256
HALF = BLOCK // 2
PIECE = 64
END_LAG = 14
END_GAP = 4
MID_LAG = 5
MID_GAP = 8
OUT_CHUNKS = 4
CHUNKS = 4
UNROLL = 2


def lane_tiles_sum(x):
    total = x[:, :LANES]
    for start in range(LANES, x.shape[1], LANES):
        total = total + x[:, start : start + LANES]
    return total


def spread(column, width):
    return jnp.concatenate([column] * (width // LANES), axis=1)


def plan(nb):
    upper = [(i, j) for i in range(nb) for j in range(i + 1, nb)]
    return upper, len(upper) // 2, nb // 2, BLOCK // PIECE, HALF // PIECE


def kernel(
    sizes, student_hbm, teacher_hbm, sbuf, pull, inv, tinv, loss_ref,
    tbuf, vbuf, shrunk, unit_low, teach_low, part, tpart,
    norms, diags, along, img_losses,
    own, prefix, ysend, yrecv, zin, zout, gathered, sqacc,
    load_sem, s_send, s_recv, d_send, d_recv, a_send, a_recv,
    i_send, i_recv, y_send, y_recv, z_send, z_recv, g_send, g_recv,
):
    n, m = sizes
    tokens, feats = unit_low.shape
    height, width = tbuf.shape[0] - 2, tbuf.shape[1]
    half_w = width // 2
    lane_tiles = feats // LANES
    nb = tokens // BLOCK
    tiles = tokens // LANES
    me = lax.axis_index("tok")
    img = lax.axis_index("img")
    col = lax.rem(me, 2)
    row = me // 2
    chain = n // 2
    upper, offs, diag, per_off, per_diag = plan(nb)
    corners = diag * per_diag
    count = corners + offs * per_off
    early = jnp.where(row < (chain + 1) // 2, 0, 1)
    late = 1 - early
    rank = jnp.minimum(row, chain - 1 - row)

    student_load = pltpu.make_async_copy(student_hbm.at[0], sbuf, load_sem.at[0])
    student_load.start()

    def load(index, first, last, to):
        copy = pltpu.make_async_copy(
            teacher_hbm.at[0, first:last],
            tbuf.at[to : to + last - first],
            load_sem.at[index],
        )
        copy.start()
        return copy

    step = height // CHUNKS
    top = load(1, 0, 1, 0)
    loads = []
    for q in range(CHUNKS):
        first = q * step + 1 if q else 0
        last = height if q == CHUNKS - 1 else (q + 1) * step + 1
        loads.append(load(3 + q, first, last, first + 1))
    bottom = load(2, height - 1, height, height + 1)

    barrier = pltpu.get_barrier_semaphore()
    for p in range(1, n):
        pl.semaphore_signal(barrier, 1, device_id={"tok": lax.rem(me + p, n)})
    for p in range(1, m):
        pl.semaphore_signal(barrier, 1, device_id={"img": lax.rem(img + p, m)})

    def gather_copies(buf, send, recv, axis, here, size):
        return [
            pltpu.make_async_remote_copy(
                src_ref=buf.at[here],
                dst_ref=buf.at[here],
                send_sem=send.at[p - 1],
                recv_sem=recv.at[p - 1],
                device_id={axis: lax.rem(here + p, size)},
            )
            for p in range(1, size)
        ]

    def pack_rows(sources):
        lane = lax.broadcasted_iota(jnp.int32, (LANES, LANES), 1)
        columns = jnp.zeros((LANES, LANES), jnp.float32)
        for k, source in enumerate(sources):
            for b in range(tiles):
                block = source[b * LANES : (b + 1) * LANES, :]
                total = jnp.sum(block, axis=1, keepdims=True)
                columns = jnp.where(lane == k * tiles + b, total, columns)
        return columns.T[: len(sources) * tiles]

    def summed(buf, size):
        total = buf[0]
        for k in range(1, size):
            total = total + buf[k]
        return total

    def unpack_rows(values, targets):
        blank = jnp.zeros((LANES - values.shape[0], LANES), jnp.float32)
        columns = jnp.concatenate([values, blank], axis=0).T
        for k, target in enumerate(targets):
            for b in range(tiles):
                at = k * tiles + b
                target[b * LANES : (b + 1) * LANES, :] = jnp.broadcast_to(
                    columns[:, at : at + 1], (LANES, LANES)
                )

    def slab(b):
        return pl.ds(pl.multiple_of(b * LANES, LANES), LANES)

    @pl.when(rank == 0)
    def _():
        zin[early] = jnp.zeros(zin.shape[1:], zin.dtype)

    sqacc[...] = jnp.zeros_like(sqacc)
    pull[...] = jnp.zeros_like(pull)
    student_load.wait()

    @pl.loop(0, tiles)
    def _(b):
        x = sbuf[slab(b), :].astype(jnp.float32)
        part[slab(b), :] = lane_tiles_sum(x * x)

    def shrink_pair(first):
        for u in range(UNROLL):
            a = first * UNROLL + u
            x = [tbuf[2 * a + k].astype(jnp.float32) for k in range(4)]
            v = cubic_taps[1] * (x[1] + x[2]) + cubic_taps[0] * (x[0] + x[3])
            for t in range(lane_tiles):
                tile = v[:, t * LANES : (t + 1) * LANES]
                vbuf[u, t, 8 : 8 + width, :] = tile
                vbuf[u, t, 7:8, :] = tile[0:1]
                vbuf[u, t, 8 + width : 9 + width, :] = tile[width - 1 : width]
        for u in range(UNROLL):
            a = first * UNROLL + u
            rows = pl.ds(pl.multiple_of(a * half_w, half_w), half_w)
            total = None
            for t in range(lane_tiles):
                w = [vbuf[u, t, pl.ds(7 + k, half_w, stride=2), :] for k in range(4)]
                h = cubic_taps[1] * (w[1] + w[2]) + cubic_taps[0] * (w[0] + w[3])
                shrunk[rows, t * LANES : (t + 1) * LANES] = h
                total = h * h if total is None else total + h * h
            tpart[rows, :] = total

    top.wait()
    for q in range(CHUNKS):
        loads[q].wait()
        if q == CHUNKS - 1:
            bottom.wait()
        trips = step // 2 // UNROLL
        pl.loop(q * trips, (q + 1) * trips)(shrink_pair)

    norms[me] = pack_rows((part, tpart))
    pl.semaphore_wait(barrier, n - 1 + m - 1)
    s_copies = gather_copies(norms, s_send, s_recv, "tok", me, n)
    for copy in s_copies:
        copy.start()
    for copy in s_copies:
        copy.wait_recv()
    unpack_rows(lax.rsqrt(summed(norms, n) + epsilon), (inv, tinv))

    @pl.loop(0, tiles)
    def _(b):
        x = sbuf[slab(b), :].astype(jnp.float32) * spread(inv[slab(b), :], feats)
        y = shrunk[slab(b), :] * spread(tinv[slab(b), :], feats)
        shrunk[slab(b), :] = x
        x = x.astype(jnp.bfloat16)
        unit_low[slab(b), :] = x
        y = y.astype(jnp.bfloat16)
        teach_low[slab(b), :] = y
        x = x.astype(jnp.float32)
        y = y.astype(jnp.float32)
        part[slab(b), :] = lane_tiles_sum(x * x - y * y)

    def strip(i):
        return pl.ds(pl.multiple_of(i * BLOCK, BLOCK), BLOCK)

    def gram(i, j):
        def product(low):
            return lax.dot_general(
                low[strip(i), :], low[strip(j), :], (((1,), (1,)), ((), ())),
                preferred_element_type=jnp.float32,
            )

        return product(unit_low) - product(teach_low)

    def pick(first, second, c):
        return tuple(p + c * (q - p) for p, q in zip(first, second))

    def off_block(k, c):
        return pick(upper[k], upper[offs + k], c)

    def diag_block(k, c):
        return 2 * k + c

    row_at = lax.broadcasted_iota(jnp.int32, (HALF, HALF), 0)
    col_at = lax.broadcasted_iota(jnp.int32, (HALF, HALF), 1)

    def fold(block):
        corner = jnp.where(row_at < col_at, block[:HALF, :HALF], block[HALF:, HALF:])
        return jnp.concatenate([corner, block[:HALF, HALF:]], axis=1)

    def y_copy(k):
        return pltpu.make_async_remote_copy(
            src_ref=ysend.at[k], dst_ref=yrecv.at[k],
            send_sem=y_send.at[k], recv_sem=y_recv.at[k],
            device_id={"tok": me + 1 - 2 * col},
        )

    def share(k, c):
        if k < diag:
            i = diag_block(k, c)
            return fold(gram(i, i)), k * per_diag, per_diag
        return gram(*off_block(k - diag, c)), corners + (k - diag) * per_off, per_off

    def give(k):
        block, first, amount = share(k, 1 - col)
        block = block.astype(jnp.bfloat16)
        for t in range(amount):
            ysend[first + t] = block[t * PIECE : (t + 1) * PIECE]
            y_copy(first + t).start()

    def keep(k):
        block, first, amount = share(k, col)
        own[first : first + amount] = block.reshape(amount, PIECE, BLOCK)

    def hop(direction):
        return {"tok": lax.rem(me + 2 - 4 * direction + n, n)}

    for k in range(offs + diag):
        give(k)
    for k in range(offs + diag):
        keep(k)
    diags[me] = pack_rows((part,))
    part[...] = jnp.zeros_like(part)
    d_copies = gather_copies(diags, d_send, d_recv, "tok", me, n)
    for copy in d_copies:
        copy.start()

    def chain_copy(direction, k):
        return pltpu.make_async_remote_copy(
            src_ref=zout.at[direction, k], dst_ref=zin.at[direction, k],
            send_sem=z_send.at[direction, k], recv_sem=z_recv.at[direction, k],
            device_id=hop(direction),
        )

    def accumulate(i, j, block):
        product = jnp.dot(block, unit_low[strip(j), :], preferred_element_type=jnp.float32)
        rows = strip(i)
        pull[rows, :] += product
        part[rows, :] += lane_tiles_sum(shrunk[rows, :] * product)

    def unfold(i, block):
        corner = block[:, :HALF].astype(jnp.float32)
        turned = corner.T
        diagonal = summed_diag(i)
        side = block[:, HALF:]

        def whole(above, below, middle):
            value = jnp.where(row_at < col_at, above, below)
            return jnp.where(row_at == col_at, middle, value).astype(jnp.bfloat16)

        top = jnp.concatenate([whole(corner, turned, diagonal[0]), side], axis=1)
        side = side.astype(jnp.float32).T.astype(jnp.bfloat16)
        low = jnp.concatenate([side, whole(turned, corner, diagonal[1])], axis=1)
        return jnp.concatenate([top, low], axis=0)

    def jobs(k, c, owner):
        amount = per_diag if k < corners else per_off
        at = k if k < corners else k - corners
        if at % amount < amount - 1:
            return []

        def block():
            rows = gathered[owner, k - amount + 1 : k + 1]
            return rows.reshape(amount * PIECE, BLOCK)

        if k < corners:
            i = diag_block(at // amount, c)
            return [lambda: accumulate(i, i, unfold(i, block()))]
        i, j = off_block(at // amount, c)
        return [
            lambda: accumulate(i, j, block()),
            lambda: accumulate(j, i, block().T),
        ]

    def summed_diag(i):
        values = []
        for t in range(2):
            total = diags[0, pl.ds(2 * i + t, 1), :]
            for k in range(1, n):
                total = total + diags[k, pl.ds(2 * i + t, 1), :]
            values.append(jnp.broadcast_to(total, (HALF, HALF)))
        return values

    def block_copy(k):
        return pltpu.make_async_remote_copy(
            src_ref=gathered.at[0, k], dst_ref=gathered.at[1, k],
            send_sem=g_send.at[k], recv_sem=g_recv.at[k],
            device_id={"tok": me + 1 - 2 * col},
        )

    def count_squares(total):
        sqacc[...] += 2.0 * jnp.sum(total * total, axis=0, keepdims=True)

    def run_early(k):
        y_copy(k).wait_recv()
        mine = own[k] + yrecv[k].astype(jnp.float32)
        copy = chain_copy(early, k)

        @pl.when(rank > 0)
        def _():
            copy.wait_recv()

        total = mine + zin[early, k].astype(jnp.float32)
        zout[early, k] = total.astype(jnp.bfloat16)
        own[k] = mine
        prefix[k] = total
        copy.start()

    def run_late(k):
        copy = chain_copy(late, k)
        copy.wait_recv()
        incoming = zin[late, k].astype(jnp.float32)
        total = prefix[k] + incoming

        @pl.when(rank > 0)
        def _():
            zout[late, k] = (own[k] + incoming).astype(jnp.bfloat16)
            copy.start()

        gathered[0, k] = total.astype(jnp.bfloat16)
        block_copy(k).start()
        if k < corners:
            first = (k % per_diag) * PIECE
            on_diagonal = row_at[:PIECE] + first == col_at[:PIECE]
            corner = jnp.where(on_diagonal, 0.0, total[:, :HALF])
            total = jnp.concatenate([corner, total[:, HALF:]], axis=1)
            if k % per_diag == 0:
                for value in summed_diag(diag_block(k // per_diag, col)):
                    sqacc[:, :HALF] += value[:1] * value[:1]
        count_squares(total)

    def run_other(k):
        block_copy(k).wait_recv()

    def await_diags():
        for copy in d_copies:
            copy.wait_recv()

    i_copies = gather_copies(img_losses, i_send, i_recv, "img", img, m)

    def send_losses():
        squared = jnp.sum(sqacc[...], axis=1, keepdims=True)
        img_losses[img] = jnp.broadcast_to(squared, img_losses.shape[1:])
        for copy in i_copies:
            copy.start()

    def run(lag, gap):
        waiting = []
        for k in range(count + lag + gap):
            if k < count:
                run_early(k)
            if k == lag:
                await_diags()
            if lag <= k < count + lag:
                run_late(k - lag)
                waiting += jobs(k - lag, col, 0)
            if k == count + lag - 1:
                send_losses()
            if lag + gap <= k:
                run_other(k - lag - gap)
                waiting += jobs(k - lag - gap, 1 - col, 1)
            if waiting:
                waiting.pop(0)()
        for job in waiting:
            job()

    @pl.when(rank == 0)
    def _():
        run(END_LAG, END_GAP)

    @pl.when(rank > 0)
    def _():
        run(MID_LAG, MID_GAP)

    for copy in i_copies:
        copy.wait_recv()
    along[me, :tiles] = pack_rows((part,))
    along[me, tiles:] = summed(img_losses, m)
    a_copies = gather_copies(along, a_send, a_recv, "tok", me, n)
    for copy in a_copies:
        copy.start()
    for copy in a_copies:
        copy.wait_recv()
    total = summed(along, n)
    unpack_rows(total[:tiles], (tinv,))
    loss_ref[...] = total[tiles:] / (chain * tokens)

    for copy in s_copies + d_copies + a_copies + i_copies:
        copy.wait_send()
    for k in range(count):
        y_copy(k).wait_send()
        block_copy(k).wait_send()
        chain_copy(early, k).wait_send()

        @pl.when(rank > 0)
        def _():
            chain_copy(late, k).wait_send()


def finish(student_ref, pull_ref, inv_ref, along_ref, loss_ref, out_hbm, total_ref, buf, sem):
    tokens, feats = pull_ref.shape
    rows = tokens // OUT_CHUNKS
    copies = []
    for b in range(OUT_CHUNKS):
        at = pl.ds(b * rows, rows)
        scale = spread(inv_ref[at, :], feats)
        unit = student_ref[at, :].astype(jnp.float32) * scale
        grad = scale * (4.0 * pull_ref[at, :])
        grad = grad - scale * unit * spread(4.0 * along_ref[at, :], feats)
        buf[at, :] = grad.astype(buf.dtype)
        copy = pltpu.make_async_copy(buf.at[at], out_hbm.at[0, at], sem.at[b])
        copy.start()
        copies.append(copy)
    total_ref[...] = loss_ref[0:1, 0:1]
    for copy in copies:
        copy.wait()


def per_device(n, m, student, teacher):
    _, tokens, feats = student.shape
    _, height, width, _ = teacher.shape
    nb = tokens // BLOCK
    _, offs, diag, per_off, per_diag = plan(nb)
    count = offs * per_off + diag * per_diag
    tiles = tokens // LANES
    f32, bf16 = jnp.float32, jnp.bfloat16
    vmem, dma = pltpu.VMEM, pltpu.SemaphoreType.DMA
    features, pull, inv, along, loss = pl.pallas_call(
        functools.partial(kernel, (n, m)),
        name="anchor",
        out_shape=(
            jax.ShapeDtypeStruct((tokens, feats), bf16),
            jax.ShapeDtypeStruct((tokens, feats), f32),
            jax.ShapeDtypeStruct((tokens, LANES), f32),
            jax.ShapeDtypeStruct((tokens, LANES), f32),
            jax.ShapeDtypeStruct((8, LANES), f32),
        ),
        in_specs=[
            pl.BlockSpec(memory_space=pltpu.HBM),
            pl.BlockSpec(memory_space=pltpu.HBM),
        ],
        out_specs=(pl.BlockSpec(memory_space=pltpu.VMEM),) * 5,
        scratch_shapes=[
            vmem((height + 2, width, feats), bf16),
            vmem((UNROLL, feats // LANES, width + 16, LANES), f32),
            vmem((tokens, feats), f32),
            vmem((tokens, feats), bf16),
            vmem((tokens, feats), bf16),
            vmem((tokens, LANES), f32),
            vmem((tokens, LANES), f32),
            vmem((n, 2 * tiles, LANES), f32),
            vmem((n, tiles, LANES), f32),
            vmem((n, tiles + 8, LANES), f32),
            vmem((m, 8, LANES), f32),
            vmem((count, PIECE, BLOCK), f32),
            vmem((count, PIECE, BLOCK), f32),
            vmem((count, PIECE, BLOCK), bf16),
            vmem((count, PIECE, BLOCK), bf16),
            vmem((2, count, PIECE, BLOCK), bf16),
            vmem((2, count, PIECE, BLOCK), bf16),
            vmem((2, count, PIECE, BLOCK), bf16),
            vmem((1, BLOCK), f32),
            dma((CHUNKS + 3,)),
            dma((n - 1,)), dma((n - 1,)), dma((n - 1,)), dma((n - 1,)),
            dma((n - 1,)), dma((n - 1,)),
            dma((m - 1,)), dma((m - 1,)),
            dma((count,)), dma((count,)),
            dma((2, count)), dma((2, count)),
            dma((count,)), dma((count,)),
        ],
        compiler_params=pltpu.CompilerParams(
            collective_id=0, has_side_effects=True, vmem_limit_bytes=32 * 1024 * 1024
        ),
    )(*(pltpu.with_memory_space_constraint(x, pltpu.HBM) for x in (student, teacher)))
    gradient, total = pl.pallas_call(
        finish,
        name="finish",
        out_shape=(
            jax.ShapeDtypeStruct(student.shape, bf16),
            jax.ShapeDtypeStruct((1, 1), f32),
        ),
        in_specs=[pl.BlockSpec(memory_space=pltpu.VMEM)] * 5,
        out_specs=(
            pl.BlockSpec(memory_space=pl.ANY),
            pl.BlockSpec(memory_space=pltpu.VMEM),
        ),
        scratch_shapes=[vmem((tokens, feats), bf16), dma((OUT_CHUNKS,))],
        compiler_params=pltpu.CompilerParams(vmem_limit_bytes=16 * 1024 * 1024),
    )(features, pull, inv, along, loss)
    return gradient, total.reshape(())


def solution(mesh):
    return jax.shard_map(
        functools.partial(per_device, mesh.shape["tok"], mesh.shape["img"]),
        mesh=mesh,
        in_specs=(P("img", None, "tok"), P("img", None, None, "tok")),
        out_specs=(P("img", None, "tok"), P()),
        check_vma=False,
    )
```

```python
import functools

import jax
import jax.numpy as jnp
from jax import lax
from jax.experimental import pallas as pl
from jax.experimental.pallas import tpu as pltpu
from jax.sharding import PartitionSpec as P

cubic_taps = (-0.09375, 0.59375, 0.59375, -0.09375)
epsilon = 1e-06
LANES = 128
BLOCK = 256
HALF = BLOCK // 2
PIECE = 64
END_LAG = 14
END_GAP = 6
MID_LAG = 5
MID_GAP = 8
OUT_CHUNKS = 4
GROUPS = 2
CHUNKS = 4
UNROLL = 2


def lane_tiles_sum(x):
    total = x[:, :LANES]
    for start in range(LANES, x.shape[1], LANES):
        total = total + x[:, start : start + LANES]
    return total


def spread(column, width):
    return jnp.concatenate([column] * (width // LANES), axis=1)


def plan(nb):
    blocks, first, count = [], [], 0
    for j in range(nb):
        for i in [j] + list(range(j)):
            blocks.append((i, j))
            first.append(count)
            count += (HALF if i < j else HALF // 2) // PIECE
    return blocks, first + [count]


def kernel(
    sizes, student_hbm, teacher_hbm, sbuf, pull, inv, tinv, loss_ref,
    tbuf, vbuf, shrunk, unit_low, teach_low, part, tpart,
    norms, diags, along, img_losses,
    own, prefix, ysend, yrecv, zin, zout, gathered, sqacc,
    load_sem, s_send, s_recv, d_send, d_recv, a_send, a_recv,
    i_send, i_recv, y_send, y_recv, z_send, z_recv, g_send, g_recv,
):
    n, m = sizes
    tokens, feats = unit_low.shape
    height, width = tbuf.shape[0] - 2, tbuf.shape[1]
    half_w = width // 2
    lane_tiles = feats // LANES
    nb = tokens // BLOCK
    tiles = tokens // LANES
    me = lax.axis_index("tok")
    img = lax.axis_index("img")
    col = lax.rem(me, 2)
    row = me // 2
    chain = n // 2
    blocks, first = plan(nb)
    count = first[-1]
    early = jnp.where(row < (chain + 1) // 2, 0, 1)
    late = 1 - early
    rank = jnp.minimum(row, chain - 1 - row)

    step, share = height // CHUNKS, tokens // CHUNKS

    def load(index, src, dst):
        copy = pltpu.make_async_copy(src, dst, load_sem.at[index])
        copy.start()
        return copy

    def load_teacher(index, low, high, to):
        return load(index, teacher_hbm.at[0, low:high], tbuf.at[to : to + high - low])

    top = load_teacher(0, 0, 1, 0)
    loads = []
    for q in range(CHUNKS):
        low = q * step + 1 if q else 0
        high = height if q == CHUNKS - 1 else (q + 1) * step + 1
        rows = slice(q * share, (q + 1) * share)
        loads.append((
            load_teacher(2 + 2 * q, low, high, low + 1),
            load(3 + 2 * q, student_hbm.at[0, rows], sbuf.at[rows]),
        ))
    bottom = load_teacher(1, height - 1, height, height + 1)

    barrier = pltpu.get_barrier_semaphore()
    for p in range(1, n):
        pl.semaphore_signal(barrier, 1, device_id={"tok": lax.rem(me + p, n)})
    for p in range(1, m):
        pl.semaphore_signal(barrier, 1, device_id={"img": lax.rem(img + p, m)})

    def gather_copies(buf, send, recv, axis, here, size):
        return [
            pltpu.make_async_remote_copy(
                src_ref=buf.at[here],
                dst_ref=buf.at[here],
                send_sem=send.at[p - 1],
                recv_sem=recv.at[p - 1],
                device_id={axis: lax.rem(here + p, size)},
            )
            for p in range(1, size)
        ]

    def pack_rows(sources, base, amount):
        lane = lax.broadcasted_iota(jnp.int32, (LANES, LANES), 1)
        columns = jnp.zeros((LANES, LANES), jnp.float32)
        for k, source in enumerate(sources):
            for b in range(amount):
                block = source[(base + b) * LANES : (base + b + 1) * LANES, :]
                total = jnp.sum(block, axis=1, keepdims=True)
                columns = jnp.where(lane == k * amount + b, total, columns)
        return columns.T[: len(sources) * amount]

    def summed(buf, size):
        total = buf[0]
        for k in range(1, size):
            total = total + buf[k]
        return total

    def unpack_rows(values, targets, base, amount):
        blank = jnp.zeros((LANES - values.shape[0], LANES), jnp.float32)
        columns = jnp.concatenate([values, blank], axis=0).T
        for k, target in enumerate(targets):
            for b in range(amount):
                at = k * amount + b
                target[(base + b) * LANES : (base + b + 1) * LANES, :] = jnp.broadcast_to(
                    columns[:, at : at + 1], (LANES, LANES)
                )

    def slab(b):
        return pl.ds(pl.multiple_of(b * LANES, LANES), LANES)

    sqacc[...] = jnp.zeros_like(sqacc)
    pull[...] = jnp.zeros_like(pull)
    def student_squares(b):
        x = sbuf[slab(b), :].astype(jnp.float32)
        part[slab(b), :] = lane_tiles_sum(x * x)

    def shrink_pair(pair):
        for u in range(UNROLL):
            a = pair * UNROLL + u
            x = [tbuf[2 * a + k].astype(jnp.float32) for k in range(4)]
            v = cubic_taps[1] * (x[1] + x[2]) + cubic_taps[0] * (x[0] + x[3])
            for t in range(lane_tiles):
                tile = v[:, t * LANES : (t + 1) * LANES]
                vbuf[u, t, 8 : 8 + width, :] = tile
                vbuf[u, t, 7:8, :] = tile[0:1]
                vbuf[u, t, 8 + width : 9 + width, :] = tile[width - 1 : width]
        for u in range(UNROLL):
            a = pair * UNROLL + u
            rows = pl.ds(pl.multiple_of(a * half_w, half_w), half_w)
            total = None
            for t in range(lane_tiles):
                w = [vbuf[u, t, pl.ds(7 + k, half_w, stride=2), :] for k in range(4)]
                h = cubic_taps[1] * (w[1] + w[2]) + cubic_taps[0] * (w[0] + w[3])
                shrunk[rows, t * LANES : (t + 1) * LANES] = h
                total = h * h if total is None else total + h * h
            tpart[rows, :] = total

    span = tiles // GROUPS
    per_group = CHUNKS // GROUPS
    s_copies = []
    top.wait()
    for q in range(CHUNKS):
        loads[q][0].wait()
        if q == CHUNKS - 1:
            bottom.wait()
        trips = step // 2 // UNROLL
        pl.loop(q * trips, (q + 1) * trips)(shrink_pair)
        loads[q][1].wait()
        pl.loop(q * share // LANES, (q + 1) * share // LANES)(student_squares)
        if q % per_group == per_group - 1:
            g = q // per_group
            norms[g, me] = pack_rows((part, tpart), g * span, span)
            if g == 0:
                pl.semaphore_wait(barrier, n - 1 + m - 1)
            s_copies.append(
                gather_copies(norms.at[g], s_send.at[g], s_recv.at[g], "tok", me, n)
            )
            for copy in s_copies[g]:
                copy.start()

    def normalise(b):
        x = sbuf[slab(b), :].astype(jnp.float32) * spread(inv[slab(b), :], feats)
        y = shrunk[slab(b), :] * spread(tinv[slab(b), :], feats)
        shrunk[slab(b), :] = x
        x = x.astype(jnp.bfloat16)
        unit_low[slab(b), :] = x
        y = y.astype(jnp.bfloat16)
        teach_low[slab(b), :] = y
        x = x.astype(jnp.float32)
        y = y.astype(jnp.float32)
        part[slab(b), :] = lane_tiles_sum(x * x - y * y)

    def await_norms(g):
        for copy in s_copies[g]:
            copy.wait_recv()
        values = lax.rsqrt(summed(norms.at[g], n) + epsilon)
        unpack_rows(values, (inv, tinv), g * span, span)
        pl.loop(g * span, (g + 1) * span)(normalise)

    def strip(i):
        return pl.ds(pl.multiple_of(i * BLOCK, BLOCK), BLOCK)

    def gram(i, j):
        def product(low):
            return lax.dot_general(
                low[strip(i), :], low[strip(j), :], (((1,), (1,)), ((), ())),
                preferred_element_type=jnp.float32,
            )

        return product(unit_low) - product(teach_low)

    row_at = lax.broadcasted_iota(jnp.int32, (HALF, HALF), 0)
    col_at = lax.broadcasted_iota(jnp.int32, (HALF, HALF), 1)

    def fold(block):
        corner = jnp.where(row_at < col_at, block[:HALF, :HALF], block[HALF:, HALF:])
        return jnp.concatenate([corner, block[:HALF, HALF:]], axis=1)

    def y_copy(k):
        return pltpu.make_async_remote_copy(
            src_ref=ysend.at[k], dst_ref=yrecv.at[k],
            send_sem=y_send.at[k], recv_sem=y_recv.at[k],
            device_id={"tok": me + 1 - 2 * col},
        )

    def give(b):
        i, j = blocks[b]
        block = gram(i, j)
        if i == j:
            block = fold(block)
        low, high = first[b], first[b + 1]
        own[:, low:high] = block.reshape(2, high - low, PIECE, BLOCK)
        for k in range(low, high):
            ysend[k] = own[1 - col, k].astype(jnp.bfloat16)
            y_copy(k).start()

    def hop(direction):
        return {"tok": lax.rem(me + 2 - 4 * direction + n, n)}

    for g in range(GROUPS):
        await_norms(g)
        for b, (i, j) in enumerate(blocks):
            if j * GROUPS // nb == g:
                give(b)
    diags[me] = pack_rows((part,), 0, tiles)
    part[...] = jnp.zeros_like(part)
    d_copies = gather_copies(diags, d_send, d_recv, "tok", me, n)
    for copy in d_copies:
        copy.start()

    def chain_copy(direction, k):
        return pltpu.make_async_remote_copy(
            src_ref=zout.at[direction, k], dst_ref=zin.at[direction, k],
            send_sem=z_send.at[direction, k], recv_sem=z_recv.at[direction, k],
            device_id=hop(direction),
        )

    def accumulate(i, j, block):
        product = jnp.dot(block, unit_low[strip(j), :], preferred_element_type=jnp.float32)
        rows = strip(i)
        pull[rows, :] += product
        part[rows, :] += lane_tiles_sum(shrunk[rows, :] * product)

    def unfold(i, block):
        corner = block[:, :HALF].astype(jnp.float32)
        turned = corner.T
        diagonal = summed_diag(i)
        side = block[:, HALF:]

        def whole(above, below, middle):
            value = jnp.where(row_at < col_at, above, below)
            return jnp.where(row_at == col_at, middle, value).astype(jnp.bfloat16)

        top = jnp.concatenate([whole(corner, turned, diagonal[0]), side], axis=1)
        side = side.astype(jnp.float32).T.astype(jnp.bfloat16)
        low = jnp.concatenate([side, whole(turned, corner, diagonal[1])], axis=1)
        return jnp.concatenate([top, low], axis=0)

    def jobs(k):
        if k + 1 not in first:
            return []
        b = first.index(k + 1) - 1
        i, j = blocks[b]

        def block():
            pieces = gathered[:, first[b] : first[b + 1]]
            return pieces.reshape(-1, BLOCK)

        if i == j:
            return [lambda: accumulate(i, i, unfold(i, block()))]
        return [
            lambda: accumulate(i, j, block()),
            lambda: accumulate(j, i, block().T),
        ]

    def summed_diag(i):
        values = []
        for t in range(2):
            total = diags[0, pl.ds(2 * i + t, 1), :]
            for k in range(1, n):
                total = total + diags[k, pl.ds(2 * i + t, 1), :]
            values.append(jnp.broadcast_to(total, (HALF, HALF)))
        return values

    def block_copy(k):
        return pltpu.make_async_remote_copy(
            src_ref=gathered.at[col, k], dst_ref=gathered.at[col, k],
            send_sem=g_send.at[k], recv_sem=g_recv.at[k],
            device_id={"tok": me + 1 - 2 * col},
        )

    def count_squares(total):
        sqacc[...] += 2.0 * jnp.sum(total * total, axis=0, keepdims=True)

    def run_early(k, outer):
        y_copy(k).wait_recv()
        mine = own[col, k] + yrecv[k].astype(jnp.float32)
        copy = chain_copy(early, k)

        total = mine
        if outer:
            copy.wait_recv()
            total = mine + zin[early, k].astype(jnp.float32)
        zout[early, k] = total.astype(jnp.bfloat16)
        own[col, k] = mine
        prefix[k] = total
        copy.start()

    def run_late(k, outer):
        copy = chain_copy(late, k)
        copy.wait_recv()
        incoming = zin[late, k].astype(jnp.float32)
        total = prefix[k] + incoming

        if outer:
            zout[late, k] = (own[col, k] + incoming).astype(jnp.bfloat16)
            copy.start()

        gathered[col, k] = total.astype(jnp.bfloat16)
        block_copy(k).start()
        b = max(x for x in range(len(blocks)) if first[x] <= k)
        i, j = blocks[b]
        if i == j:
            offset = col * (HALF // 2) + (k - first[b]) * PIECE
            on_diagonal = row_at[:PIECE] + offset == col_at[:PIECE]
            corner = jnp.where(on_diagonal, 0.0, total[:, :HALF])
            total = jnp.concatenate([corner, total[:, HALF:]], axis=1)
            if k == first[b]:
                for value in summed_diag(i):
                    sqacc[:, :HALF] += 0.5 * value[:1] * value[:1]
        count_squares(total)

    def run_other(k):
        block_copy(k).wait_recv()

    def await_diags():
        for copy in d_copies:
            copy.wait_recv()

    i_copies = gather_copies(img_losses, i_send, i_recv, "img", img, m)

    def send_losses():
        squared = jnp.sum(sqacc[...], axis=1, keepdims=True)
        img_losses[img] = jnp.broadcast_to(squared, img_losses.shape[1:])
        for copy in i_copies:
            copy.start()

    def run(lag, gap, outer):
        waiting = []
        for k in range(count + lag + gap):
            if k < count:
                run_early(k, outer)
            if k == lag:
                await_diags()
            if lag <= k < count + lag:
                run_late(k - lag, outer)
            if k == count + lag - 1:
                send_losses()
            if lag + gap <= k:
                run_other(k - lag - gap)
                waiting += jobs(k - lag - gap)
            if waiting:
                waiting.pop(0)()
        for job in waiting:
            job()

    @pl.when(rank == 0)
    def _():
        run(END_LAG, END_GAP, False)

    @pl.when(rank > 0)
    def _():
        run(MID_LAG, MID_GAP, True)

    for copy in i_copies:
        copy.wait_recv()
    along[me, :tiles] = pack_rows((part,), 0, tiles)
    along[me, tiles:] = summed(img_losses, m)
    a_copies = gather_copies(along, a_send, a_recv, "tok", me, n)
    for copy in a_copies:
        copy.start()
    for copy in a_copies:
        copy.wait_recv()
    total = summed(along, n)
    unpack_rows(total[:tiles], (tinv,), 0, tiles)
    loss_ref[...] = total[tiles:] / (chain * tokens)

    for copy in sum(s_copies, []) + d_copies + a_copies + i_copies:
        copy.wait_send()
    for k in range(count):
        y_copy(k).wait_send()
        block_copy(k).wait_send()
        chain_copy(early, k).wait_send()

        @pl.when(rank > 0)
        def _():
            chain_copy(late, k).wait_send()


def finish(student_ref, pull_ref, inv_ref, along_ref, loss_ref, out_hbm, total_ref, buf, sem):
    tokens, feats = pull_ref.shape
    rows = tokens // OUT_CHUNKS
    copies = []
    for b in range(OUT_CHUNKS):
        at = pl.ds(b * rows, rows)
        scale = spread(inv_ref[at, :], feats)
        unit = student_ref[at, :].astype(jnp.float32) * scale
        grad = scale * (4.0 * pull_ref[at, :])
        grad = grad - scale * unit * spread(4.0 * along_ref[at, :], feats)
        buf[at, :] = grad.astype(buf.dtype)
        copy = pltpu.make_async_copy(buf.at[at], out_hbm.at[0, at], sem.at[b])
        copy.start()
        copies.append(copy)
    total_ref[...] = loss_ref[0:1, 0:1]
    for copy in copies:
        copy.wait()


def per_device(n, m, student, teacher):
    _, tokens, feats = student.shape
    _, height, width, _ = teacher.shape
    nb = tokens // BLOCK
    count = plan(nb)[1][-1]
    tiles = tokens // LANES
    f32, bf16 = jnp.float32, jnp.bfloat16
    vmem, dma = pltpu.VMEM, pltpu.SemaphoreType.DMA
    features, pull, inv, along, loss = pl.pallas_call(
        functools.partial(kernel, (n, m)),
        name="anchor",
        out_shape=(
            jax.ShapeDtypeStruct((tokens, feats), bf16),
            jax.ShapeDtypeStruct((tokens, feats), f32),
            jax.ShapeDtypeStruct((tokens, LANES), f32),
            jax.ShapeDtypeStruct((tokens, LANES), f32),
            jax.ShapeDtypeStruct((8, LANES), f32),
        ),
        in_specs=[
            pl.BlockSpec(memory_space=pltpu.HBM),
            pl.BlockSpec(memory_space=pltpu.HBM),
        ],
        out_specs=(pl.BlockSpec(memory_space=pltpu.VMEM),) * 5,
        scratch_shapes=[
            vmem((height + 2, width, feats), bf16),
            vmem((UNROLL, feats // LANES, width + 16, LANES), f32),
            vmem((tokens, feats), f32),
            vmem((tokens, feats), bf16),
            vmem((tokens, feats), bf16),
            vmem((tokens, LANES), f32),
            vmem((tokens, LANES), f32),
            vmem((GROUPS, n, 2 * tiles // GROUPS, LANES), f32),
            vmem((n, tiles, LANES), f32),
            vmem((n, tiles + 8, LANES), f32),
            vmem((m, 8, LANES), f32),
            vmem((2, count, PIECE, BLOCK), f32),
            vmem((count, PIECE, BLOCK), f32),
            vmem((count, PIECE, BLOCK), bf16),
            vmem((count, PIECE, BLOCK), bf16),
            vmem((2, count, PIECE, BLOCK), bf16),
            vmem((2, count, PIECE, BLOCK), bf16),
            vmem((2, count, PIECE, BLOCK), bf16),
            vmem((1, BLOCK), f32),
            dma((2 * CHUNKS + 2,)),
            dma((GROUPS, n - 1)), dma((GROUPS, n - 1)), dma((n - 1,)), dma((n - 1,)),
            dma((n - 1,)), dma((n - 1,)),
            dma((m - 1,)), dma((m - 1,)),
            dma((count,)), dma((count,)),
            dma((2, count)), dma((2, count)),
            dma((count,)), dma((count,)),
        ],
        compiler_params=pltpu.CompilerParams(
            collective_id=0, has_side_effects=True, vmem_limit_bytes=32 * 1024 * 1024
        ),
    )(*(pltpu.with_memory_space_constraint(x, pltpu.HBM) for x in (student, teacher)))
    gradient, total = pl.pallas_call(
        finish,
        name="finish",
        out_shape=(
            jax.ShapeDtypeStruct(student.shape, bf16),
            jax.ShapeDtypeStruct((1, 1), f32),
        ),
        in_specs=[pl.BlockSpec(memory_space=pltpu.VMEM)] * 5,
        out_specs=(
            pl.BlockSpec(memory_space=pl.ANY),
            pl.BlockSpec(memory_space=pltpu.VMEM),
        ),
        scratch_shapes=[vmem((tokens, feats), bf16), dma((OUT_CHUNKS,))],
        compiler_params=pltpu.CompilerParams(vmem_limit_bytes=16 * 1024 * 1024),
    )(features, pull, inv, along, loss)
    return gradient, total.reshape(())


def solution(mesh):
    return jax.shard_map(
        functools.partial(per_device, mesh.shape["tok"], mesh.shape["img"]),
        mesh=mesh,
        in_specs=(P("img", None, "tok"), P("img", None, None, "tok")),
        out_specs=(P("img", None, "tok"), P()),
        check_vma=False,
    )
```

```python
import functools

import jax
import jax.numpy as jnp
from jax import lax
from jax.experimental import pallas as pl
from jax.experimental.pallas import tpu as pltpu
from jax.sharding import PartitionSpec as P

cubic_taps = (-0.09375, 0.59375, 0.59375, -0.09375)
epsilon = 1e-06
LANES = 128
BLOCK = 256
HALF = BLOCK // 2
PIECE = 64
END_LAG = 16
END_GAP = 6
MID_LAG = 5
MID_GAP = 8
QUICK = 1
OUT_CHUNKS = 4
GROUPS = 2
CHUNKS = 4
UNROLL = 2


def lane_tiles_sum(x):
    total = x[:, :LANES]
    for start in range(LANES, x.shape[1], LANES):
        total = total + x[:, start : start + LANES]
    return total


def spread(column, width):
    return jnp.concatenate([column] * (width // LANES), axis=1)


def plan(nb):
    quick = [(0, j) for j in range(1, nb)][:QUICK]
    blocks = list(quick)
    for j in range(nb):
        blocks += [(i, j) for i in [j] + list(range(j)) if (i, j) not in quick]
    first = [0]
    for i, j in blocks:
        first.append(first[-1] + (HALF if i < j else HALF // 2) // PIECE)
    return blocks, first, len(quick)


def kernel(
    sizes, student_hbm, teacher_hbm, sbuf, pull, inv, tinv, loss_ref,
    tbuf, vbuf, shrunk, unit_low, teach_low, part, tpart,
    norms, diags, along, img_losses,
    own, prefix, ysend, yrecv, qsend, qrecv, factors, zin, zout, gathered, sqacc,
    load_sem, s_send, s_recv, d_send, d_recv, a_send, a_recv,
    i_send, i_recv, y_send, y_recv, q_send, q_recv, z_send, z_recv, g_send, g_recv,
):
    n, m = sizes
    tokens, feats = unit_low.shape
    height, width = tbuf.shape[0] - 2, tbuf.shape[1]
    half_w = width // 2
    lane_tiles = feats // LANES
    nb = tokens // BLOCK
    tiles = tokens // LANES
    me = lax.axis_index("tok")
    img = lax.axis_index("img")
    col = lax.rem(me, 2)
    row = me // 2
    chain = n // 2
    blocks, first, quick = plan(nb)
    count = first[-1]
    early = jnp.where(row < (chain + 1) // 2, 0, 1)
    late = 1 - early
    rank = jnp.minimum(row, chain - 1 - row)

    barrier = pltpu.get_barrier_semaphore()
    for p in range(1, n):
        pl.semaphore_signal(barrier, 1, device_id={"tok": lax.rem(me + p, n)})
    for p in range(1, m):
        pl.semaphore_signal(barrier, 1, device_id={"img": lax.rem(img + p, m)})

    step, share = height // CHUNKS, tokens // CHUNKS

    def load(index, src, dst):
        copy = pltpu.make_async_copy(src, dst, load_sem.at[index])
        copy.start()
        return copy

    def load_teacher(index, low, high, to):
        return load(index, teacher_hbm.at[0, low:high], tbuf.at[to : to + high - low])

    top = load_teacher(0, 0, 1, 0)
    loads = []
    for q in range(CHUNKS):
        low = q * step + 1 if q else 0
        high = height if q == CHUNKS - 1 else (q + 1) * step + 1
        rows = slice(q * share, (q + 1) * share)
        loads.append((
            load_teacher(2 + 2 * q, low, high, low + 1),
            load(3 + 2 * q, student_hbm.at[0, rows], sbuf.at[rows]),
        ))
    bottom = load_teacher(1, height - 1, height, height + 1)

    def gather_copies(buf, send, recv, axis, here, size):
        return [
            pltpu.make_async_remote_copy(
                src_ref=buf.at[here],
                dst_ref=buf.at[here],
                send_sem=send.at[p - 1],
                recv_sem=recv.at[p - 1],
                device_id={axis: lax.rem(here + p, size)},
            )
            for p in range(1, size)
        ]

    def pack_rows(sources, base, amount):
        lane = lax.broadcasted_iota(jnp.int32, (LANES, LANES), 1)
        columns = jnp.zeros((LANES, LANES), jnp.float32)
        for k, source in enumerate(sources):
            for b in range(amount):
                block = source[(base + b) * LANES : (base + b + 1) * LANES, :]
                total = jnp.sum(block, axis=1, keepdims=True)
                columns = jnp.where(lane == k * amount + b, total, columns)
        return columns.T[: len(sources) * amount]

    def summed(buf, size):
        total = buf[0]
        for k in range(1, size):
            total = total + buf[k]
        return total

    def unpack_rows(values, targets, base, amount):
        blank = jnp.zeros((LANES - values.shape[0], LANES), jnp.float32)
        columns = jnp.concatenate([values, blank], axis=0).T
        for k, target in enumerate(targets):
            for b in range(amount):
                at = k * amount + b
                target[(base + b) * LANES : (base + b + 1) * LANES, :] = jnp.broadcast_to(
                    columns[:, at : at + 1], (LANES, LANES)
                )

    def slab(b):
        return pl.ds(pl.multiple_of(b * LANES, LANES), LANES)

    sqacc[...] = jnp.zeros_like(sqacc)
    pull[...] = jnp.zeros_like(pull)
    def student_squares(b):
        x = sbuf[slab(b), :].astype(jnp.float32)
        part[slab(b), :] = lane_tiles_sum(x * x)

    def shrink_pair(pair):
        for u in range(UNROLL):
            a = pair * UNROLL + u
            x = [tbuf[2 * a + k].astype(jnp.float32) for k in range(4)]
            v = cubic_taps[1] * (x[1] + x[2]) + cubic_taps[0] * (x[0] + x[3])
            for t in range(lane_tiles):
                tile = v[:, t * LANES : (t + 1) * LANES]
                vbuf[u, t, 8 : 8 + width, :] = tile
                vbuf[u, t, 7:8, :] = tile[0:1]
                vbuf[u, t, 8 + width : 9 + width, :] = tile[width - 1 : width]
        for u in range(UNROLL):
            a = pair * UNROLL + u
            rows = pl.ds(pl.multiple_of(a * half_w, half_w), half_w)
            total = None
            for t in range(lane_tiles):
                w = [vbuf[u, t, pl.ds(7 + k, half_w, stride=2), :] for k in range(4)]
                h = cubic_taps[1] * (w[1] + w[2]) + cubic_taps[0] * (w[0] + w[3])
                shrunk[rows, t * LANES : (t + 1) * LANES] = h
                teach_low[rows, t * LANES : (t + 1) * LANES] = h.astype(jnp.bfloat16)
                total = h * h if total is None else total + h * h
            tpart[rows, :] = total

    span = tiles // GROUPS
    per_group = CHUNKS // GROUPS
    s_copies = []
    top.wait()
    for q in range(CHUNKS):
        loads[q][0].wait()
        if q == CHUNKS - 1:
            bottom.wait()
        trips = step // 2 // UNROLL
        pl.loop(q * trips, (q + 1) * trips)(shrink_pair)
        loads[q][1].wait()
        pl.loop(q * share // LANES, (q + 1) * share // LANES)(student_squares)
        if q % per_group == per_group - 1:
            g = q // per_group
            norms[g, me] = pack_rows((part, tpart), g * span, span)
            if g == 0:
                pl.semaphore_wait(barrier, n - 1 + m - 1)
            s_copies.append(
                gather_copies(norms.at[g], s_send.at[g], s_recv.at[g], "tok", me, n)
            )
            for copy in s_copies[g]:
                copy.start()

    def normalise(b):
        x = sbuf[slab(b), :].astype(jnp.float32) * spread(inv[slab(b), :], feats)
        y = shrunk[slab(b), :] * spread(tinv[slab(b), :], feats)
        shrunk[slab(b), :] = x
        x = x.astype(jnp.bfloat16)
        unit_low[slab(b), :] = x
        y = y.astype(jnp.bfloat16)
        teach_low[slab(b), :] = y
        x = x.astype(jnp.float32)
        y = y.astype(jnp.float32)
        part[slab(b), :] = lane_tiles_sum(x * x - y * y)

    def await_norms(g):
        for copy in s_copies[g]:
            copy.wait_recv()
        values = lax.rsqrt(summed(norms.at[g], n) + epsilon)
        factors[g] = values
        unpack_rows(values, (inv, tinv), g * span, span)
        pl.loop(g * span, (g + 1) * span)(normalise)

    def strip(i):
        return pl.ds(pl.multiple_of(i * BLOCK, BLOCK), BLOCK)

    def gram(i, j):
        def product(low):
            return lax.dot_general(
                low[strip(i), :], low[strip(j), :], (((1,), (1,)), ((), ())),
                preferred_element_type=jnp.float32,
            )

        return product(unit_low) - product(teach_low)

    row_at = lax.broadcasted_iota(jnp.int32, (HALF, HALF), 0)
    col_at = lax.broadcasted_iota(jnp.int32, (HALF, HALF), 1)

    def fold(block):
        corner = jnp.where(row_at < col_at, block[:HALF, :HALF], block[HALF:, HALF:])
        return jnp.concatenate([corner, block[:HALF, HALF:]], axis=1)

    def y_copy(k):
        return pltpu.make_async_remote_copy(
            src_ref=ysend.at[k], dst_ref=yrecv.at[k],
            send_sem=y_send.at[k], recv_sem=y_recv.at[k],
            device_id={"tok": me + 1 - 2 * col},
        )

    def half(i, c):
        return pl.ds(pl.multiple_of(i * BLOCK + c * HALF, HALF), HALF)

    def half_gram(low, i, j, c):
        return lax.dot_general(
            low[half(i, c), :], low[strip(j), :], (((1,), (1,)), ((), ())),
            preferred_element_type=jnp.float32,
        )

    def quick_copy(b, s):
        return pltpu.make_async_remote_copy(
            src_ref=qsend.at[s, b], dst_ref=qrecv.at[s, b],
            send_sem=q_send.at[s, b], recv_sem=q_recv.at[s, b],
            device_id={"tok": me + 1 - 2 * col},
        )

    def scaled(b, t, s):
        i, j = blocks[b]
        column = (inv, tinv)[s]
        start = i * BLOCK + col * HALF + t * PIECE
        rows = pl.ds(pl.multiple_of(start, PIECE), PIECE)
        tile = j * (BLOCK // LANES)
        at = s * span + tile % span
        across = [
            factors[tile // span, at + x : at + x + 1, :] for x in range(BLOCK // LANES)
        ]
        values = qrecv[s, b, t * PIECE : (t + 1) * PIECE].astype(jnp.float32)
        values = values * spread(column[rows, :], BLOCK)
        return values * jnp.concatenate(across, axis=1)

    def give(b):
        i, j = blocks[b]
        low, high = first[b], first[b + 1]
        if b < quick:
            block = half_gram(unit_low, i, j, col) - half_gram(teach_low, i, j, col)
            own[col, low:high] = block.reshape(high - low, PIECE, BLOCK)
            return
        block = gram(i, j)
        if i == j:
            block = fold(block)
        own[:, low:high] = block.reshape(2, high - low, PIECE, BLOCK)
        for k in range(low, high):
            ysend[k] = own[1 - col, k].astype(jnp.bfloat16)
            y_copy(k).start()

    def hop(direction):
        return {"tok": lax.rem(me + 2 - 4 * direction + n, n)}

    for b in range(quick):
        for s, low in enumerate((sbuf, teach_low)):
            qsend[s, b] = half_gram(low, *blocks[b], 1 - col).astype(jnp.bfloat16)
            quick_copy(b, s).start()

    for g in range(GROUPS):
        await_norms(g)
        ready = [b for b, (i, j) in enumerate(blocks) if j * GROUPS // nb == g]
        for b in sorted(ready, key=lambda b: b < quick):
            give(b)
    diags[me] = pack_rows((part,), 0, tiles)
    part[...] = jnp.zeros_like(part)
    d_copies = gather_copies(diags, d_send, d_recv, "tok", me, n)
    for copy in d_copies:
        copy.start()

    def chain_copy(direction, k):
        return pltpu.make_async_remote_copy(
            src_ref=zout.at[direction, k], dst_ref=zin.at[direction, k],
            send_sem=z_send.at[direction, k], recv_sem=z_recv.at[direction, k],
            device_id=hop(direction),
        )

    def accumulate(i, j, block):
        product = jnp.dot(block, unit_low[strip(j), :], preferred_element_type=jnp.float32)
        rows = strip(i)
        pull[rows, :] += product
        part[rows, :] += lane_tiles_sum(shrunk[rows, :] * product)

    def unfold(i, block):
        corner = block[:, :HALF].astype(jnp.float32)
        turned = corner.T
        diagonal = summed_diag(i)
        side = block[:, HALF:]

        def whole(above, below, middle):
            value = jnp.where(row_at < col_at, above, below)
            return jnp.where(row_at == col_at, middle, value).astype(jnp.bfloat16)

        top = jnp.concatenate([whole(corner, turned, diagonal[0]), side], axis=1)
        side = side.astype(jnp.float32).T.astype(jnp.bfloat16)
        low = jnp.concatenate([side, whole(turned, corner, diagonal[1])], axis=1)
        return jnp.concatenate([top, low], axis=0)

    def jobs(k):
        if k + 1 not in first:
            return []
        b = first.index(k + 1) - 1
        i, j = blocks[b]

        def block():
            pieces = gathered[:, first[b] : first[b + 1]]
            return pieces.reshape(-1, BLOCK)

        if i == j:
            return [lambda: accumulate(i, i, unfold(i, block()))]
        return [
            lambda: accumulate(i, j, block()),
            lambda: accumulate(j, i, block().T),
        ]

    def summed_diag(i):
        values = []
        for t in range(2):
            total = diags[0, pl.ds(2 * i + t, 1), :]
            for k in range(1, n):
                total = total + diags[k, pl.ds(2 * i + t, 1), :]
            values.append(jnp.broadcast_to(total, (HALF, HALF)))
        return values

    def block_copy(k):
        return pltpu.make_async_remote_copy(
            src_ref=gathered.at[col, k], dst_ref=gathered.at[col, k],
            send_sem=g_send.at[k], recv_sem=g_recv.at[k],
            device_id={"tok": me + 1 - 2 * col},
        )

    def count_squares(total):
        sqacc[...] += 2.0 * jnp.sum(total * total, axis=0, keepdims=True)

    def run_early(k, outer):
        if k < first[quick]:
            b = max(x for x in range(quick) if first[x] <= k)
            if k == first[b]:
                for s in range(2):
                    quick_copy(b, s).wait_recv()
            t = k - first[b]
            mine = own[col, k] + (scaled(b, t, 0) - scaled(b, t, 1))
        else:
            y_copy(k).wait_recv()
            mine = own[col, k] + yrecv[k].astype(jnp.float32)
        copy = chain_copy(early, k)

        total = mine
        if outer:
            copy.wait_recv()
            total = mine + zin[early, k].astype(jnp.float32)
        zout[early, k] = total.astype(jnp.bfloat16)
        own[col, k] = mine
        prefix[k] = total
        copy.start()

    def run_late(k, outer):
        copy = chain_copy(late, k)
        copy.wait_recv()
        incoming = zin[late, k].astype(jnp.float32)
        total = prefix[k] + incoming

        if outer:
            zout[late, k] = (own[col, k] + incoming).astype(jnp.bfloat16)
            copy.start()

        gathered[col, k] = total.astype(jnp.bfloat16)
        block_copy(k).start()
        b = max(x for x in range(len(blocks)) if first[x] <= k)
        i, j = blocks[b]
        if i == j:
            offset = col * (HALF // 2) + (k - first[b]) * PIECE
            on_diagonal = row_at[:PIECE] + offset == col_at[:PIECE]
            corner = jnp.where(on_diagonal, 0.0, total[:, :HALF])
            total = jnp.concatenate([corner, total[:, HALF:]], axis=1)
            if k == first[b]:
                for value in summed_diag(i):
                    sqacc[:, :HALF] += 0.5 * value[:1] * value[:1]
        count_squares(total)

    def run_other(k):
        block_copy(k).wait_recv()

    def await_diags():
        for copy in d_copies:
            copy.wait_recv()

    i_copies = gather_copies(img_losses, i_send, i_recv, "img", img, m)

    def send_losses():
        squared = jnp.sum(sqacc[...], axis=1, keepdims=True)
        img_losses[img] = jnp.broadcast_to(squared, img_losses.shape[1:])
        for copy in i_copies:
            copy.start()

    def run(lag, gap, outer):
        waiting = []
        for k in range(count + lag + gap):
            if k < count:
                run_early(k, outer)
            if k == lag:
                await_diags()
            if lag <= k < count + lag:
                run_late(k - lag, outer)
            if k == count + lag - 1:
                send_losses()
            if lag + gap <= k:
                run_other(k - lag - gap)
                waiting += jobs(k - lag - gap)
            if waiting:
                waiting.pop(0)()
        for job in waiting:
            job()

    @pl.when(rank == 0)
    def _():
        run(END_LAG, END_GAP, False)

    @pl.when(rank > 0)
    def _():
        run(MID_LAG, MID_GAP, True)

    for copy in i_copies:
        copy.wait_recv()
    along[me, :tiles] = pack_rows((part,), 0, tiles)
    along[me, tiles:] = summed(img_losses, m)
    a_copies = gather_copies(along, a_send, a_recv, "tok", me, n)
    for copy in a_copies:
        copy.start()
    for copy in a_copies:
        copy.wait_recv()
    total = summed(along, n)
    unpack_rows(total[:tiles], (tinv,), 0, tiles)
    loss_ref[...] = total[tiles:] / (chain * tokens)

    for copy in sum(s_copies, []) + d_copies + a_copies + i_copies:
        copy.wait_send()
    for b in range(quick):
        for s in range(2):
            quick_copy(b, s).wait_send()
    for k in range(count):
        if k >= first[quick]:
            y_copy(k).wait_send()
        block_copy(k).wait_send()
        chain_copy(early, k).wait_send()

        @pl.when(rank > 0)
        def _():
            chain_copy(late, k).wait_send()


def finish(student_ref, pull_ref, inv_ref, along_ref, loss_ref, out_hbm, total_ref, buf, sem):
    tokens, feats = pull_ref.shape
    rows = tokens // OUT_CHUNKS
    copies = []
    for b in range(OUT_CHUNKS):
        at = pl.ds(b * rows, rows)
        scale = spread(inv_ref[at, :], feats)
        unit = student_ref[at, :].astype(jnp.float32) * scale
        grad = scale * (4.0 * pull_ref[at, :])
        grad = grad - scale * unit * spread(4.0 * along_ref[at, :], feats)
        buf[at, :] = grad.astype(buf.dtype)
        copy = pltpu.make_async_copy(buf.at[at], out_hbm.at[0, at], sem.at[b])
        copy.start()
        copies.append(copy)
    total_ref[...] = loss_ref[0:1, 0:1]
    for copy in copies:
        copy.wait()


def per_device(n, m, student, teacher):
    _, tokens, feats = student.shape
    _, height, width, _ = teacher.shape
    nb = tokens // BLOCK
    _, first, quick = plan(nb)
    count = first[-1]
    tiles = tokens // LANES
    f32, bf16 = jnp.float32, jnp.bfloat16
    vmem, dma = pltpu.VMEM, pltpu.SemaphoreType.DMA
    features, pull, inv, along, loss = pl.pallas_call(
        functools.partial(kernel, (n, m)),
        name="anchor",
        out_shape=(
            jax.ShapeDtypeStruct((tokens, feats), bf16),
            jax.ShapeDtypeStruct((tokens, feats), f32),
            jax.ShapeDtypeStruct((tokens, LANES), f32),
            jax.ShapeDtypeStruct((tokens, LANES), f32),
            jax.ShapeDtypeStruct((8, LANES), f32),
        ),
        in_specs=[
            pl.BlockSpec(memory_space=pltpu.HBM),
            pl.BlockSpec(memory_space=pltpu.HBM),
        ],
        out_specs=(pl.BlockSpec(memory_space=pltpu.VMEM),) * 5,
        scratch_shapes=[
            vmem((height + 2, width, feats), bf16),
            vmem((UNROLL, feats // LANES, width + 16, LANES), f32),
            vmem((tokens, feats), f32),
            vmem((tokens, feats), bf16),
            vmem((tokens, feats), bf16),
            vmem((tokens, LANES), f32),
            vmem((tokens, LANES), f32),
            vmem((GROUPS, n, 2 * tiles // GROUPS, LANES), f32),
            vmem((n, tiles, LANES), f32),
            vmem((n, tiles + 8, LANES), f32),
            vmem((m, 8, LANES), f32),
            vmem((2, count, PIECE, BLOCK), f32),
            vmem((count, PIECE, BLOCK), f32),
            vmem((count, PIECE, BLOCK), bf16),
            vmem((count, PIECE, BLOCK), bf16),
            vmem((2, quick, HALF, BLOCK), bf16),
            vmem((2, quick, HALF, BLOCK), bf16),
            vmem((GROUPS, 2 * tiles // GROUPS, LANES), f32),
            vmem((2, count, PIECE, BLOCK), bf16),
            vmem((2, count, PIECE, BLOCK), bf16),
            vmem((2, count, PIECE, BLOCK), bf16),
            vmem((1, BLOCK), f32),
            dma((2 * CHUNKS + 2,)),
            dma((GROUPS, n - 1)), dma((GROUPS, n - 1)), dma((n - 1,)), dma((n - 1,)),
            dma((n - 1,)), dma((n - 1,)),
            dma((m - 1,)), dma((m - 1,)),
            dma((count,)), dma((count,)),
            dma((2, quick)), dma((2, quick)),
            dma((2, count)), dma((2, count)),
            dma((count,)), dma((count,)),
        ],
        compiler_params=pltpu.CompilerParams(
            collective_id=0, has_side_effects=True, vmem_limit_bytes=32 * 1024 * 1024
        ),
    )(*(pltpu.with_memory_space_constraint(x, pltpu.HBM) for x in (student, teacher)))
    gradient, total = pl.pallas_call(
        finish,
        name="finish",
        out_shape=(
            jax.ShapeDtypeStruct(student.shape, bf16),
            jax.ShapeDtypeStruct((1, 1), f32),
        ),
        in_specs=[pl.BlockSpec(memory_space=pltpu.VMEM)] * 5,
        out_specs=(
            pl.BlockSpec(memory_space=pl.ANY),
            pl.BlockSpec(memory_space=pltpu.VMEM),
        ),
        scratch_shapes=[vmem((tokens, feats), bf16), dma((OUT_CHUNKS,))],
        compiler_params=pltpu.CompilerParams(vmem_limit_bytes=16 * 1024 * 1024),
    )(features, pull, inv, along, loss)
    return gradient, total.reshape(())


def solution(mesh):
    return jax.shard_map(
        functools.partial(per_device, mesh.shape["tok"], mesh.shape["img"]),
        mesh=mesh,
        in_specs=(P("img", None, "tok"), P("img", None, None, "tok")),
        out_specs=(P("img", None, "tok"), P()),
        check_vma=False,
    )
```

```python
import functools

import jax
import jax.numpy as jnp
from jax import lax
from jax.experimental import pallas as pl
from jax.experimental.pallas import tpu as pltpu
from jax.sharding import PartitionSpec as P

cubic_taps = (-0.09375, 0.59375, 0.59375, -0.09375)
epsilon = 1e-06
LANES = 128
BLOCK = 256
HALF = BLOCK // 2
PIECE = 64
END_LAG = 16
END_GAP = 8
MID_LAG = 5
MID_GAP = 8
QUICK = 1
OUT_CHUNKS = 8
GROUPS = 2
CHUNKS = 4
UNROLL = 2


def lane_tiles_sum(x):
    total = x[:, :LANES]
    for start in range(LANES, x.shape[1], LANES):
        total = total + x[:, start : start + LANES]
    return total


def spread(column, width):
    return jnp.concatenate([column] * (width // LANES), axis=1)


def plan(nb):
    quick = [(0, j) for j in range(1, nb)][:QUICK]
    blocks = list(quick)
    for j in range(nb):
        blocks += [(i, j) for i in [j] + list(range(j)) if (i, j) not in quick]
    first = [0]
    for i, j in blocks:
        first.append(first[-1] + (HALF if i < j else HALF // 2) // PIECE)
    return blocks, first, len(quick)


def kernel(
    sizes, student_hbm, teacher_hbm, sbuf, pull, inv, tinv, loss_ref,
    tbuf, vbuf, shrunk, unit_low, teach_low, part, tpart,
    norms, diags, along, img_losses,
    own, prefix, ysend, yrecv, qsend, qrecv, factors, zin, zout, gathered, sqacc,
    load_sem, s_send, s_recv, d_send, d_recv, a_send, a_recv,
    i_send, i_recv, y_send, y_recv, q_send, q_recv, z_send, z_recv, g_send, g_recv,
):
    n, m = sizes
    tokens, feats = unit_low.shape
    height, width = tbuf.shape[0] - 2, tbuf.shape[1]
    half_w = width // 2
    lane_tiles = feats // LANES
    nb = tokens // BLOCK
    tiles = tokens // LANES
    me = lax.axis_index("tok")
    img = lax.axis_index("img")
    col = lax.rem(me, 2)
    row = me // 2
    chain = n // 2
    blocks, first, quick = plan(nb)
    count = first[-1]
    early = jnp.where(row < (chain + 1) // 2, 0, 1)
    late = 1 - early
    rank = jnp.minimum(row, chain - 1 - row)

    barrier = pltpu.get_barrier_semaphore()
    for p in range(1, n):
        pl.semaphore_signal(barrier, 1, device_id={"tok": lax.rem(me + p, n)})
    for p in range(1, m):
        pl.semaphore_signal(barrier, 1, device_id={"img": lax.rem(img + p, m)})

    step, share = height // CHUNKS, tokens // CHUNKS

    def load(index, src, dst):
        copy = pltpu.make_async_copy(src, dst, load_sem.at[index])
        copy.start()
        return copy

    def load_teacher(index, low, high, to):
        return load(index, teacher_hbm.at[0, low:high], tbuf.at[to : to + high - low])

    top = load_teacher(0, 0, 1, 0)
    loads = []
    for q in range(CHUNKS):
        low = q * step + 1 if q else 0
        high = height if q == CHUNKS - 1 else (q + 1) * step + 1
        rows = slice(q * share, (q + 1) * share)
        loads.append((
            load_teacher(2 + 2 * q, low, high, low + 1),
            load(3 + 2 * q, student_hbm.at[0, rows], sbuf.at[rows]),
        ))
    bottom = load_teacher(1, height - 1, height, height + 1)

    def gather_copies(buf, send, recv, axis, here, size):
        return [
            pltpu.make_async_remote_copy(
                src_ref=buf.at[here],
                dst_ref=buf.at[here],
                send_sem=send.at[p - 1],
                recv_sem=recv.at[p - 1],
                device_id={axis: lax.rem(here + p, size)},
            )
            for p in range(1, size)
        ]

    def pack_rows(sources, base, amount):
        lane = lax.broadcasted_iota(jnp.int32, (LANES, LANES), 1)
        columns = jnp.zeros((LANES, LANES), jnp.float32)
        for k, source in enumerate(sources):
            for b in range(amount):
                block = source[(base + b) * LANES : (base + b + 1) * LANES, :]
                total = jnp.sum(block, axis=1, keepdims=True)
                columns = jnp.where(lane == k * amount + b, total, columns)
        return columns.T[: len(sources) * amount]

    def summed(buf, size):
        total = buf[0]
        for k in range(1, size):
            total = total + buf[k]
        return total

    def unpack_rows(values, targets, base, amount):
        blank = jnp.zeros((LANES - values.shape[0], LANES), jnp.float32)
        columns = jnp.concatenate([values, blank], axis=0).T
        for k, target in enumerate(targets):
            for b in range(amount):
                at = k * amount + b
                target[(base + b) * LANES : (base + b + 1) * LANES, :] = jnp.broadcast_to(
                    columns[:, at : at + 1], (LANES, LANES)
                )

    def slab(b):
        return pl.ds(pl.multiple_of(b * LANES, LANES), LANES)

    sqacc[...] = jnp.zeros_like(sqacc)
    pull[...] = jnp.zeros_like(pull)
    def student_squares(b):
        x = sbuf[slab(b), :].astype(jnp.float32)
        part[slab(b), :] = lane_tiles_sum(x * x)

    def shrink_pair(pair):
        for u in range(UNROLL):
            a = pair * UNROLL + u
            x = [tbuf[2 * a + k].astype(jnp.float32) for k in range(4)]
            v = cubic_taps[1] * (x[1] + x[2]) + cubic_taps[0] * (x[0] + x[3])
            for t in range(lane_tiles):
                tile = v[:, t * LANES : (t + 1) * LANES]
                vbuf[u, t, 8 : 8 + width, :] = tile
                vbuf[u, t, 7:8, :] = tile[0:1]
                vbuf[u, t, 8 + width : 9 + width, :] = tile[width - 1 : width]
        for u in range(UNROLL):
            a = pair * UNROLL + u
            rows = pl.ds(pl.multiple_of(a * half_w, half_w), half_w)
            total = None
            for t in range(lane_tiles):
                w = [vbuf[u, t, pl.ds(7 + k, half_w, stride=2), :] for k in range(4)]
                h = cubic_taps[1] * (w[1] + w[2]) + cubic_taps[0] * (w[0] + w[3])
                shrunk[rows, t * LANES : (t + 1) * LANES] = h
                teach_low[rows, t * LANES : (t + 1) * LANES] = h.astype(jnp.bfloat16)
                total = h * h if total is None else total + h * h
            tpart[rows, :] = total

    span = tiles // GROUPS
    per_group = CHUNKS // GROUPS
    s_copies = []
    top.wait()
    for q in range(CHUNKS):
        loads[q][0].wait()
        if q == CHUNKS - 1:
            bottom.wait()
        trips = step // 2 // UNROLL
        pl.loop(q * trips, (q + 1) * trips)(shrink_pair)
        loads[q][1].wait()
        pl.loop(q * share // LANES, (q + 1) * share // LANES)(student_squares)
        if q % per_group == per_group - 1:
            g = q // per_group
            norms[g, me] = pack_rows((part, tpart), g * span, span)
            if g == 0:
                pl.semaphore_wait(barrier, n - 1 + m - 1)
            s_copies.append(
                gather_copies(norms.at[g], s_send.at[g], s_recv.at[g], "tok", me, n)
            )
            for copy in s_copies[g]:
                copy.start()

    def normalise(b):
        x = sbuf[slab(b), :].astype(jnp.float32) * spread(inv[slab(b), :], feats)
        y = shrunk[slab(b), :] * spread(tinv[slab(b), :], feats)
        shrunk[slab(b), :] = x
        x = x.astype(jnp.bfloat16)
        unit_low[slab(b), :] = x
        y = y.astype(jnp.bfloat16)
        teach_low[slab(b), :] = y
        x = x.astype(jnp.float32)
        y = y.astype(jnp.float32)
        part[slab(b), :] = lane_tiles_sum(x * x - y * y)

    def await_norms(g):
        for copy in s_copies[g]:
            copy.wait_recv()
        values = lax.rsqrt(summed(norms.at[g], n) + epsilon)
        factors[g] = values
        unpack_rows(values, (inv, tinv), g * span, span)
        pl.loop(g * span, (g + 1) * span)(normalise)

    def strip(i):
        return pl.ds(pl.multiple_of(i * BLOCK, BLOCK), BLOCK)

    def gram(i, j):
        def product(low):
            return lax.dot_general(
                low[strip(i), :], low[strip(j), :], (((1,), (1,)), ((), ())),
                preferred_element_type=jnp.float32,
            )

        return product(unit_low) - product(teach_low)

    row_at = lax.broadcasted_iota(jnp.int32, (HALF, HALF), 0)
    col_at = lax.broadcasted_iota(jnp.int32, (HALF, HALF), 1)

    def fold(block):
        corner = jnp.where(row_at < col_at, block[:HALF, :HALF], block[HALF:, HALF:])
        return jnp.concatenate([corner, block[:HALF, HALF:]], axis=1)

    def y_copy(k):
        return pltpu.make_async_remote_copy(
            src_ref=ysend.at[k], dst_ref=yrecv.at[k],
            send_sem=y_send.at[k], recv_sem=y_recv.at[k],
            device_id={"tok": me + 1 - 2 * col},
        )

    def half(i, c):
        return pl.ds(pl.multiple_of(i * BLOCK + c * HALF, HALF), HALF)

    def half_gram(low, i, j, c):
        return lax.dot_general(
            low[half(i, c), :], low[strip(j), :], (((1,), (1,)), ((), ())),
            preferred_element_type=jnp.float32,
        )

    def quick_copy(b, s):
        return pltpu.make_async_remote_copy(
            src_ref=qsend.at[s, b], dst_ref=qrecv.at[s, b],
            send_sem=q_send.at[s, b], recv_sem=q_recv.at[s, b],
            device_id={"tok": me + 1 - 2 * col},
        )

    def scaled(b, t, s):
        i, j = blocks[b]
        column = (inv, tinv)[s]
        start = i * BLOCK + col * HALF + t * PIECE
        rows = pl.ds(pl.multiple_of(start, PIECE), PIECE)
        tile = j * (BLOCK // LANES)
        at = s * span + tile % span
        across = [
            factors[tile // span, at + x : at + x + 1, :] for x in range(BLOCK // LANES)
        ]
        values = qrecv[s, b, t * PIECE : (t + 1) * PIECE].astype(jnp.float32)
        values = values * spread(column[rows, :], BLOCK)
        return values * jnp.concatenate(across, axis=1)

    def give(b):
        i, j = blocks[b]
        low, high = first[b], first[b + 1]
        if b < quick:
            block = half_gram(unit_low, i, j, col) - half_gram(teach_low, i, j, col)
            own[col, low:high] = block.reshape(high - low, PIECE, BLOCK)
            return
        block = gram(i, j)
        if i == j:
            block = fold(block)
        own[:, low:high] = block.reshape(2, high - low, PIECE, BLOCK)
        for k in range(low, high):
            ysend[k] = own[1 - col, k].astype(jnp.bfloat16)
            y_copy(k).start()

    def hop(direction):
        return {"tok": lax.rem(me + 2 - 4 * direction + n, n)}

    for b in range(quick):
        for s, low in enumerate((sbuf, teach_low)):
            qsend[s, b] = half_gram(low, *blocks[b], 1 - col).astype(jnp.bfloat16)
            quick_copy(b, s).start()

    for g in range(GROUPS):
        await_norms(g)
        ready = [b for b, (i, j) in enumerate(blocks) if j * GROUPS // nb == g]
        for b in sorted(ready, key=lambda b: b < quick):
            give(b)
    diags[me] = pack_rows((part,), 0, tiles)
    part[...] = jnp.zeros_like(part)
    d_copies = gather_copies(diags, d_send, d_recv, "tok", me, n)
    for copy in d_copies:
        copy.start()

    def chain_copy(direction, k):
        return pltpu.make_async_remote_copy(
            src_ref=zout.at[direction, k], dst_ref=zin.at[direction, k],
            send_sem=z_send.at[direction, k], recv_sem=z_recv.at[direction, k],
            device_id=hop(direction),
        )

    def accumulate(i, j, block):
        product = jnp.dot(block, unit_low[strip(j), :], preferred_element_type=jnp.float32)
        rows = strip(i)
        pull[rows, :] += product
        part[rows, :] += lane_tiles_sum(shrunk[rows, :] * product)

    def unfold(i, block):
        corner = block[:, :HALF].astype(jnp.float32)
        turned = corner.T
        diagonal = summed_diag(i)
        side = block[:, HALF:]

        def whole(above, below, middle):
            value = jnp.where(row_at < col_at, above, below)
            return jnp.where(row_at == col_at, middle, value).astype(jnp.bfloat16)

        top = jnp.concatenate([whole(corner, turned, diagonal[0]), side], axis=1)
        side = side.astype(jnp.float32).T.astype(jnp.bfloat16)
        low = jnp.concatenate([side, whole(turned, corner, diagonal[1])], axis=1)
        return jnp.concatenate([top, low], axis=0)

    def jobs(k):
        if k + 1 not in first:
            return []
        b = first.index(k + 1) - 1
        i, j = blocks[b]

        def block():
            pieces = gathered[:, first[b] : first[b + 1]]
            return pieces.reshape(-1, BLOCK)

        if i == j:
            return [lambda: accumulate(i, i, unfold(i, block()))]
        return [
            lambda: accumulate(i, j, block()),
            lambda: accumulate(j, i, block().T),
        ]

    def summed_diag(i):
        values = []
        for t in range(2):
            total = diags[0, pl.ds(2 * i + t, 1), :]
            for k in range(1, n):
                total = total + diags[k, pl.ds(2 * i + t, 1), :]
            values.append(jnp.broadcast_to(total, (HALF, HALF)))
        return values

    def block_copy(k):
        return pltpu.make_async_remote_copy(
            src_ref=gathered.at[col, k], dst_ref=gathered.at[col, k],
            send_sem=g_send.at[k], recv_sem=g_recv.at[k],
            device_id={"tok": me + 1 - 2 * col},
        )

    def count_squares(total):
        sqacc[...] += 2.0 * jnp.sum(total * total, axis=0, keepdims=True)

    def run_early(k, outer):
        if k < first[quick]:
            b = max(x for x in range(quick) if first[x] <= k)
            if k == first[b]:
                for s in range(2):
                    quick_copy(b, s).wait_recv()
            t = k - first[b]
            mine = own[col, k] + (scaled(b, t, 0) - scaled(b, t, 1))
        else:
            y_copy(k).wait_recv()
            mine = own[col, k] + yrecv[k].astype(jnp.float32)
        copy = chain_copy(early, k)

        total = mine
        if outer:
            copy.wait_recv()
            total = mine + zin[early, k].astype(jnp.float32)
        zout[early, k] = total.astype(jnp.bfloat16)
        own[col, k] = mine
        prefix[k] = total
        copy.start()

    def run_late(k, outer):
        copy = chain_copy(late, k)
        copy.wait_recv()
        incoming = zin[late, k].astype(jnp.float32)
        total = prefix[k] + incoming

        if outer:
            zout[late, k] = (own[col, k] + incoming).astype(jnp.bfloat16)
            copy.start()

        gathered[col, k] = total.astype(jnp.bfloat16)
        block_copy(k).start()
        b = max(x for x in range(len(blocks)) if first[x] <= k)
        i, j = blocks[b]
        if i == j:
            offset = col * (HALF // 2) + (k - first[b]) * PIECE
            on_diagonal = row_at[:PIECE] + offset == col_at[:PIECE]
            corner = jnp.where(on_diagonal, 0.0, total[:, :HALF])
            total = jnp.concatenate([corner, total[:, HALF:]], axis=1)
            if k == first[b]:
                for value in summed_diag(i):
                    sqacc[:, :HALF] += 0.5 * value[:1] * value[:1]
        count_squares(total)

    def run_other(k):
        block_copy(k).wait_recv()

    def await_diags():
        for copy in d_copies:
            copy.wait_recv()

    i_copies = gather_copies(img_losses, i_send, i_recv, "img", img, m)

    def send_losses():
        squared = jnp.sum(sqacc[...], axis=1, keepdims=True)
        img_losses[img] = jnp.broadcast_to(squared, img_losses.shape[1:])
        for copy in i_copies:
            copy.start()

    def run(lag, gap, outer):
        waiting = []
        for k in range(count + lag + gap):
            if k < count:
                run_early(k, outer)
            if k == lag:
                await_diags()
            if lag <= k < count + lag:
                run_late(k - lag, outer)
            if k == count + lag - 1:
                send_losses()
            if lag + gap <= k:
                run_other(k - lag - gap)
                waiting += jobs(k - lag - gap)
            if waiting:
                waiting.pop(0)()
        for job in waiting:
            job()

    @pl.when(rank == 0)
    def _():
        run(END_LAG, END_GAP, False)

    @pl.when(rank > 0)
    def _():
        run(MID_LAG, MID_GAP, True)

    for copy in i_copies:
        copy.wait_recv()
    along[me, :tiles] = pack_rows((part,), 0, tiles)
    along[me, tiles:] = summed(img_losses, m)
    a_copies = gather_copies(along, a_send, a_recv, "tok", me, n)
    for copy in a_copies:
        copy.start()
    for copy in a_copies:
        copy.wait_recv()
    total = summed(along, n)
    unpack_rows(total[:tiles], (tinv,), 0, tiles)
    loss_ref[...] = total[tiles:] / (chain * tokens)

    for copy in sum(s_copies, []) + d_copies + a_copies + i_copies:
        copy.wait_send()
    for b in range(quick):
        for s in range(2):
            quick_copy(b, s).wait_send()
    for k in range(count):
        if k >= first[quick]:
            y_copy(k).wait_send()
        block_copy(k).wait_send()
        chain_copy(early, k).wait_send()

        @pl.when(rank > 0)
        def _():
            chain_copy(late, k).wait_send()


def finish(student_ref, pull_ref, inv_ref, along_ref, loss_ref, out_hbm, total_ref, buf, sem):
    tokens, feats = pull_ref.shape
    rows = tokens // OUT_CHUNKS
    copies = []
    for b in range(OUT_CHUNKS):
        at = pl.ds(b * rows, rows)
        scale = spread(inv_ref[at, :], feats)
        unit = student_ref[at, :].astype(jnp.float32) * scale
        grad = scale * (4.0 * pull_ref[at, :])
        grad = grad - scale * unit * spread(4.0 * along_ref[at, :], feats)
        buf[at, :] = grad.astype(buf.dtype)
        copy = pltpu.make_async_copy(buf.at[at], out_hbm.at[0, at], sem.at[b])
        copy.start()
        copies.append(copy)
    total_ref[...] = loss_ref[0:1, 0:1]
    for copy in copies:
        copy.wait()


def per_device(n, m, student, teacher):
    _, tokens, feats = student.shape
    _, height, width, _ = teacher.shape
    nb = tokens // BLOCK
    _, first, quick = plan(nb)
    count = first[-1]
    tiles = tokens // LANES
    f32, bf16 = jnp.float32, jnp.bfloat16
    vmem, dma = pltpu.VMEM, pltpu.SemaphoreType.DMA
    features, pull, inv, along, loss = pl.pallas_call(
        functools.partial(kernel, (n, m)),
        name="anchor",
        out_shape=(
            jax.ShapeDtypeStruct((tokens, feats), bf16),
            jax.ShapeDtypeStruct((tokens, feats), f32),
            jax.ShapeDtypeStruct((tokens, LANES), f32),
            jax.ShapeDtypeStruct((tokens, LANES), f32),
            jax.ShapeDtypeStruct((8, LANES), f32),
        ),
        in_specs=[
            pl.BlockSpec(memory_space=pltpu.HBM),
            pl.BlockSpec(memory_space=pltpu.HBM),
        ],
        out_specs=(pl.BlockSpec(memory_space=pltpu.VMEM),) * 5,
        scratch_shapes=[
            vmem((height + 2, width, feats), bf16),
            vmem((UNROLL, feats // LANES, width + 16, LANES), f32),
            vmem((tokens, feats), f32),
            vmem((tokens, feats), bf16),
            vmem((tokens, feats), bf16),
            vmem((tokens, LANES), f32),
            vmem((tokens, LANES), f32),
            vmem((GROUPS, n, 2 * tiles // GROUPS, LANES), f32),
            vmem((n, tiles, LANES), f32),
            vmem((n, tiles + 8, LANES), f32),
            vmem((m, 8, LANES), f32),
            vmem((2, count, PIECE, BLOCK), f32),
            vmem((count, PIECE, BLOCK), f32),
            vmem((count, PIECE, BLOCK), bf16),
            vmem((count, PIECE, BLOCK), bf16),
            vmem((2, quick, HALF, BLOCK), bf16),
            vmem((2, quick, HALF, BLOCK), bf16),
            vmem((GROUPS, 2 * tiles // GROUPS, LANES), f32),
            vmem((2, count, PIECE, BLOCK), bf16),
            vmem((2, count, PIECE, BLOCK), bf16),
            vmem((2, count, PIECE, BLOCK), bf16),
            vmem((1, BLOCK), f32),
            dma((2 * CHUNKS + 2,)),
            dma((GROUPS, n - 1)), dma((GROUPS, n - 1)), dma((n - 1,)), dma((n - 1,)),
            dma((n - 1,)), dma((n - 1,)),
            dma((m - 1,)), dma((m - 1,)),
            dma((count,)), dma((count,)),
            dma((2, quick)), dma((2, quick)),
            dma((2, count)), dma((2, count)),
            dma((count,)), dma((count,)),
        ],
        compiler_params=pltpu.CompilerParams(
            collective_id=0, has_side_effects=True, vmem_limit_bytes=32 * 1024 * 1024
        ),
    )(*(pltpu.with_memory_space_constraint(x, pltpu.HBM) for x in (student, teacher)))
    gradient, total = pl.pallas_call(
        finish,
        name="finish",
        out_shape=(
            jax.ShapeDtypeStruct(student.shape, bf16),
            jax.ShapeDtypeStruct((1, 1), f32),
        ),
        in_specs=[pl.BlockSpec(memory_space=pltpu.VMEM)] * 5,
        out_specs=(
            pl.BlockSpec(memory_space=pl.ANY),
            pl.BlockSpec(memory_space=pltpu.VMEM),
        ),
        scratch_shapes=[vmem((tokens, feats), bf16), dma((OUT_CHUNKS,))],
        compiler_params=pltpu.CompilerParams(vmem_limit_bytes=16 * 1024 * 1024),
    )(features, pull, inv, along, loss)
    return gradient, total.reshape(())


def solution(mesh):
    return jax.shard_map(
        functools.partial(per_device, mesh.shape["tok"], mesh.shape["img"]),
        mesh=mesh,
        in_specs=(P("img", None, "tok"), P("img", None, None, "tok")),
        out_specs=(P("img", None, "tok"), P()),
        check_vma=False,
    )
```

```python
import functools

import jax
import jax.numpy as jnp
from jax import lax
from jax.experimental import pallas as pl
from jax.experimental.pallas import tpu as pltpu
from jax.sharding import PartitionSpec as P

cubic_taps = (-0.09375, 0.59375, 0.59375, -0.09375)
epsilon = 1e-06
LANES = 128
BLOCK = 256
HALF = BLOCK // 2
PIECE = 64
END_LAG = 16
END_GAP = 8
MID_LAG = 5
MID_GAP = 8
QUICK = 1
OUT_CHUNKS = 8
GROUPS = 2
CHUNKS = 4
UNROLL = 4


def lane_tiles_sum(x):
    total = x[:, :LANES]
    for start in range(LANES, x.shape[1], LANES):
        total = total + x[:, start : start + LANES]
    return total


def spread(column, width):
    return jnp.concatenate([column] * (width // LANES), axis=1)


def plan(nb):
    quick = [(0, j) for j in range(1, nb)][:QUICK]
    blocks = list(quick)
    for j in range(nb):
        blocks += [(i, j) for i in [j] + list(range(j)) if (i, j) not in quick]
    first = [0]
    for i, j in blocks:
        first.append(first[-1] + (HALF if i < j else HALF // 2) // PIECE)
    return blocks, first, len(quick)


def kernel(
    sizes, student_hbm, teacher_hbm, sbuf, pull, inv, tinv, loss_ref,
    tbuf, vbuf, shrunk, unit_low, teach_low, part, tpart,
    norms, diags, along, img_losses,
    own, prefix, ysend, yrecv, qsend, qrecv, factors, zin, zout, gathered, sqacc,
    load_sem, s_send, s_recv, d_send, d_recv, a_send, a_recv,
    i_send, i_recv, y_send, y_recv, q_send, q_recv, z_send, z_recv, g_send, g_recv,
):
    n, m = sizes
    tokens, feats = unit_low.shape
    height, width = tbuf.shape[0] - 2, tbuf.shape[1]
    half_w = width // 2
    lane_tiles = feats // LANES
    nb = tokens // BLOCK
    tiles = tokens // LANES
    me = lax.axis_index("tok")
    img = lax.axis_index("img")
    col = lax.rem(me, 2)
    row = me // 2
    chain = n // 2
    blocks, first, quick = plan(nb)
    count = first[-1]
    early = jnp.where(row < (chain + 1) // 2, 0, 1)
    late = 1 - early
    rank = jnp.minimum(row, chain - 1 - row)

    barrier = pltpu.get_barrier_semaphore()
    for p in range(1, n):
        pl.semaphore_signal(barrier, 1, device_id={"tok": lax.rem(me + p, n)})
    for p in range(1, m):
        pl.semaphore_signal(barrier, 1, device_id={"img": lax.rem(img + p, m)})

    step, share = height // CHUNKS, tokens // CHUNKS

    def load(index, src, dst):
        copy = pltpu.make_async_copy(src, dst, load_sem.at[index])
        copy.start()
        return copy

    def load_teacher(index, low, high, to):
        return load(index, teacher_hbm.at[0, low:high], tbuf.at[to : to + high - low])

    top = load_teacher(0, 0, 1, 0)
    loads = []
    for q in range(CHUNKS):
        low = q * step + 1 if q else 0
        high = height if q == CHUNKS - 1 else (q + 1) * step + 1
        rows = slice(q * share, (q + 1) * share)
        loads.append((
            load_teacher(2 + 2 * q, low, high, low + 1),
            load(3 + 2 * q, student_hbm.at[0, rows], sbuf.at[rows]),
        ))
    bottom = load_teacher(1, height - 1, height, height + 1)

    def gather_copies(buf, send, recv, axis, here, size):
        return [
            pltpu.make_async_remote_copy(
                src_ref=buf.at[here],
                dst_ref=buf.at[here],
                send_sem=send.at[p - 1],
                recv_sem=recv.at[p - 1],
                device_id={axis: lax.rem(here + p, size)},
            )
            for p in range(1, size)
        ]

    def pack_rows(sources, base, amount):
        lane = lax.broadcasted_iota(jnp.int32, (LANES, LANES), 1)
        columns = jnp.zeros((LANES, LANES), jnp.float32)
        for k, source in enumerate(sources):
            for b in range(amount):
                block = source[(base + b) * LANES : (base + b + 1) * LANES, :]
                total = jnp.sum(block, axis=1, keepdims=True)
                columns = jnp.where(lane == k * amount + b, total, columns)
        return columns.T[: len(sources) * amount]

    def summed(buf, size):
        total = buf[0]
        for k in range(1, size):
            total = total + buf[k]
        return total

    def unpack_rows(values, targets, base, amount):
        blank = jnp.zeros((LANES - values.shape[0], LANES), jnp.float32)
        columns = jnp.concatenate([values, blank], axis=0).T
        for k, target in enumerate(targets):
            for b in range(amount):
                at = k * amount + b
                target[(base + b) * LANES : (base + b + 1) * LANES, :] = jnp.broadcast_to(
                    columns[:, at : at + 1], (LANES, LANES)
                )

    def slab(b):
        return pl.ds(pl.multiple_of(b * LANES, LANES), LANES)

    sqacc[...] = jnp.zeros_like(sqacc)
    pull[...] = jnp.zeros_like(pull)
    def student_squares(b):
        x = sbuf[slab(b), :].astype(jnp.float32)
        part[slab(b), :] = lane_tiles_sum(x * x)

    def shrink_pair(pair):
        for u in range(UNROLL):
            a = pair * UNROLL + u
            x = [tbuf[2 * a + k].astype(jnp.float32) for k in range(4)]
            v = cubic_taps[1] * (x[1] + x[2]) + cubic_taps[0] * (x[0] + x[3])
            for t in range(lane_tiles):
                tile = v[:, t * LANES : (t + 1) * LANES]
                vbuf[u, t, 8 : 8 + width, :] = tile
                vbuf[u, t, 7:8, :] = tile[0:1]
                vbuf[u, t, 8 + width : 9 + width, :] = tile[width - 1 : width]
        for u in range(UNROLL):
            a = pair * UNROLL + u
            rows = pl.ds(pl.multiple_of(a * half_w, half_w), half_w)
            total = None
            for t in range(lane_tiles):
                w = [vbuf[u, t, pl.ds(7 + k, half_w, stride=2), :] for k in range(4)]
                h = cubic_taps[1] * (w[1] + w[2]) + cubic_taps[0] * (w[0] + w[3])
                shrunk[rows, t * LANES : (t + 1) * LANES] = h
                teach_low[rows, t * LANES : (t + 1) * LANES] = h.astype(jnp.bfloat16)
                total = h * h if total is None else total + h * h
            tpart[rows, :] = total

    span = tiles // GROUPS
    per_group = CHUNKS // GROUPS
    s_copies = []
    top.wait()
    for q in range(CHUNKS):
        loads[q][0].wait()
        if q == CHUNKS - 1:
            bottom.wait()
        trips = step // 2 // UNROLL
        pl.loop(q * trips, (q + 1) * trips)(shrink_pair)
        loads[q][1].wait()
        pl.loop(q * share // LANES, (q + 1) * share // LANES)(student_squares)
        if q % per_group == per_group - 1:
            g = q // per_group
            norms[g, me] = pack_rows((part, tpart), g * span, span)
            if g == 0:
                pl.semaphore_wait(barrier, n - 1 + m - 1)
            s_copies.append(
                gather_copies(norms.at[g], s_send.at[g], s_recv.at[g], "tok", me, n)
            )
            for copy in s_copies[g]:
                copy.start()

    def normalise(b):
        x = sbuf[slab(b), :].astype(jnp.float32) * spread(inv[slab(b), :], feats)
        y = shrunk[slab(b), :] * spread(tinv[slab(b), :], feats)
        shrunk[slab(b), :] = x
        x = x.astype(jnp.bfloat16)
        unit_low[slab(b), :] = x
        y = y.astype(jnp.bfloat16)
        teach_low[slab(b), :] = y
        x = x.astype(jnp.float32)
        y = y.astype(jnp.float32)
        part[slab(b), :] = lane_tiles_sum(x * x - y * y)

    def await_norms(g):
        for copy in s_copies[g]:
            copy.wait_recv()
        values = lax.rsqrt(summed(norms.at[g], n) + epsilon)
        factors[g] = values
        unpack_rows(values, (inv, tinv), g * span, span)
        pl.loop(g * span, (g + 1) * span)(normalise)

    def strip(i):
        return pl.ds(pl.multiple_of(i * BLOCK, BLOCK), BLOCK)

    def gram(i, j):
        def product(low):
            return lax.dot_general(
                low[strip(i), :], low[strip(j), :], (((1,), (1,)), ((), ())),
                preferred_element_type=jnp.float32,
            )

        return product(unit_low) - product(teach_low)

    row_at = lax.broadcasted_iota(jnp.int32, (HALF, HALF), 0)
    col_at = lax.broadcasted_iota(jnp.int32, (HALF, HALF), 1)

    def fold(block):
        corner = jnp.where(row_at < col_at, block[:HALF, :HALF], block[HALF:, HALF:])
        return jnp.concatenate([corner, block[:HALF, HALF:]], axis=1)

    def y_copy(k):
        return pltpu.make_async_remote_copy(
            src_ref=ysend.at[k], dst_ref=yrecv.at[k],
            send_sem=y_send.at[k], recv_sem=y_recv.at[k],
            device_id={"tok": me + 1 - 2 * col},
        )

    def half(i, c):
        return pl.ds(pl.multiple_of(i * BLOCK + c * HALF, HALF), HALF)

    def half_gram(low, i, j, c):
        return lax.dot_general(
            low[half(i, c), :], low[strip(j), :], (((1,), (1,)), ((), ())),
            preferred_element_type=jnp.float32,
        )

    def quick_copy(b, s):
        return pltpu.make_async_remote_copy(
            src_ref=qsend.at[s, b], dst_ref=qrecv.at[s, b],
            send_sem=q_send.at[s, b], recv_sem=q_recv.at[s, b],
            device_id={"tok": me + 1 - 2 * col},
        )

    def scaled(b, t, s):
        i, j = blocks[b]
        column = (inv, tinv)[s]
        start = i * BLOCK + col * HALF + t * PIECE
        rows = pl.ds(pl.multiple_of(start, PIECE), PIECE)
        tile = j * (BLOCK // LANES)
        at = s * span + tile % span
        across = [
            factors[tile // span, at + x : at + x + 1, :] for x in range(BLOCK // LANES)
        ]
        values = qrecv[s, b, t * PIECE : (t + 1) * PIECE].astype(jnp.float32)
        values = values * spread(column[rows, :], BLOCK)
        return values * jnp.concatenate(across, axis=1)

    def give(b):
        i, j = blocks[b]
        low, high = first[b], first[b + 1]
        if b < quick:
            block = half_gram(unit_low, i, j, col) - half_gram(teach_low, i, j, col)
            own[col, low:high] = block.reshape(high - low, PIECE, BLOCK)
            return
        block = gram(i, j)
        if i == j:
            block = fold(block)
        own[:, low:high] = block.reshape(2, high - low, PIECE, BLOCK)
        for k in range(low, high):
            ysend[k] = own[1 - col, k].astype(jnp.bfloat16)
            y_copy(k).start()

    def hop(direction):
        return {"tok": lax.rem(me + 2 - 4 * direction + n, n)}

    for b in range(quick):
        for s, low in enumerate((sbuf, teach_low)):
            qsend[s, b] = half_gram(low, *blocks[b], 1 - col).astype(jnp.bfloat16)
            quick_copy(b, s).start()

    for g in range(GROUPS):
        await_norms(g)
        ready = [b for b, (i, j) in enumerate(blocks) if j * GROUPS // nb == g]
        for b in sorted(ready, key=lambda b: b < quick):
            give(b)
    diags[me] = pack_rows((part,), 0, tiles)
    part[...] = jnp.zeros_like(part)
    d_copies = gather_copies(diags, d_send, d_recv, "tok", me, n)
    for copy in d_copies:
        copy.start()

    def chain_copy(direction, k):
        return pltpu.make_async_remote_copy(
            src_ref=zout.at[direction, k], dst_ref=zin.at[direction, k],
            send_sem=z_send.at[direction, k], recv_sem=z_recv.at[direction, k],
            device_id=hop(direction),
        )

    def accumulate(i, j, block):
        product = jnp.dot(block, unit_low[strip(j), :], preferred_element_type=jnp.float32)
        rows = strip(i)
        pull[rows, :] += product
        part[rows, :] += lane_tiles_sum(shrunk[rows, :] * product)

    def unfold(i, block):
        corner = block[:, :HALF].astype(jnp.float32)
        turned = corner.T
        diagonal = summed_diag(i)
        side = block[:, HALF:]

        def whole(above, below, middle):
            value = jnp.where(row_at < col_at, above, below)
            return jnp.where(row_at == col_at, middle, value).astype(jnp.bfloat16)

        top = jnp.concatenate([whole(corner, turned, diagonal[0]), side], axis=1)
        side = side.astype(jnp.float32).T.astype(jnp.bfloat16)
        low = jnp.concatenate([side, whole(turned, corner, diagonal[1])], axis=1)
        return jnp.concatenate([top, low], axis=0)

    def jobs(k):
        if k + 1 not in first:
            return []
        b = first.index(k + 1) - 1
        i, j = blocks[b]

        def block():
            pieces = gathered[:, first[b] : first[b + 1]]
            return pieces.reshape(-1, BLOCK)

        if i == j:
            return [lambda: accumulate(i, i, unfold(i, block()))]
        return [
            lambda: accumulate(i, j, block()),
            lambda: accumulate(j, i, block().T),
        ]

    def summed_diag(i):
        values = []
        for t in range(2):
            total = diags[0, pl.ds(2 * i + t, 1), :]
            for k in range(1, n):
                total = total + diags[k, pl.ds(2 * i + t, 1), :]
            values.append(jnp.broadcast_to(total, (HALF, HALF)))
        return values

    def block_copy(k):
        return pltpu.make_async_remote_copy(
            src_ref=gathered.at[col, k], dst_ref=gathered.at[col, k],
            send_sem=g_send.at[k], recv_sem=g_recv.at[k],
            device_id={"tok": me + 1 - 2 * col},
        )

    def count_squares(total):
        sqacc[...] += 2.0 * jnp.sum(total * total, axis=0, keepdims=True)

    def run_early(k, outer):
        if k < first[quick]:
            b = max(x for x in range(quick) if first[x] <= k)
            if k == first[b]:
                for s in range(2):
                    quick_copy(b, s).wait_recv()
            t = k - first[b]
            mine = own[col, k] + (scaled(b, t, 0) - scaled(b, t, 1))
        else:
            y_copy(k).wait_recv()
            mine = own[col, k] + yrecv[k].astype(jnp.float32)
        copy = chain_copy(early, k)

        total = mine
        if outer:
            copy.wait_recv()
            total = mine + zin[early, k].astype(jnp.float32)
        zout[early, k] = total.astype(jnp.bfloat16)
        own[col, k] = mine
        prefix[k] = total
        copy.start()

    def run_late(k, outer):
        copy = chain_copy(late, k)
        copy.wait_recv()
        incoming = zin[late, k].astype(jnp.float32)
        total = prefix[k] + incoming

        if outer:
            zout[late, k] = (own[col, k] + incoming).astype(jnp.bfloat16)
            copy.start()

        gathered[col, k] = total.astype(jnp.bfloat16)
        block_copy(k).start()
        b = max(x for x in range(len(blocks)) if first[x] <= k)
        i, j = blocks[b]
        if i == j:
            offset = col * (HALF // 2) + (k - first[b]) * PIECE
            on_diagonal = row_at[:PIECE] + offset == col_at[:PIECE]
            corner = jnp.where(on_diagonal, 0.0, total[:, :HALF])
            total = jnp.concatenate([corner, total[:, HALF:]], axis=1)
            if k == first[b]:
                for value in summed_diag(i):
                    sqacc[:, :HALF] += 0.5 * value[:1] * value[:1]
        count_squares(total)

    def run_other(k):
        block_copy(k).wait_recv()

    def await_diags():
        for copy in d_copies:
            copy.wait_recv()

    i_copies = gather_copies(img_losses, i_send, i_recv, "img", img, m)

    def send_losses():
        squared = jnp.sum(sqacc[...], axis=1, keepdims=True)
        img_losses[img] = jnp.broadcast_to(squared, img_losses.shape[1:])
        for copy in i_copies:
            copy.start()

    def run(lag, gap, outer):
        waiting = []
        for k in range(count + lag + gap):
            if k < count:
                run_early(k, outer)
            if k == lag:
                await_diags()
            if lag <= k < count + lag:
                run_late(k - lag, outer)
            if k == count + lag - 1:
                send_losses()
            if lag + gap <= k:
                run_other(k - lag - gap)
                waiting += jobs(k - lag - gap)
            if waiting:
                waiting.pop(0)()
        for job in waiting:
            job()

    @pl.when(rank == 0)
    def _():
        run(END_LAG, END_GAP, False)

    @pl.when(rank > 0)
    def _():
        run(MID_LAG, MID_GAP, True)

    for copy in i_copies:
        copy.wait_recv()
    along[me, :tiles] = pack_rows((part,), 0, tiles)
    along[me, tiles:] = summed(img_losses, m)
    a_copies = gather_copies(along, a_send, a_recv, "tok", me, n)
    for copy in a_copies:
        copy.start()
    for copy in a_copies:
        copy.wait_recv()
    total = summed(along, n)
    unpack_rows(total[:tiles], (tinv,), 0, tiles)
    loss_ref[...] = total[tiles:] / (chain * tokens)

    for copy in sum(s_copies, []) + d_copies + a_copies + i_copies:
        copy.wait_send()
    for b in range(quick):
        for s in range(2):
            quick_copy(b, s).wait_send()
    for k in range(count):
        if k >= first[quick]:
            y_copy(k).wait_send()
        block_copy(k).wait_send()
        chain_copy(early, k).wait_send()

        @pl.when(rank > 0)
        def _():
            chain_copy(late, k).wait_send()


def finish(student_ref, pull_ref, inv_ref, along_ref, loss_ref, out_hbm, total_ref, buf, sem):
    tokens, feats = pull_ref.shape
    rows = tokens // OUT_CHUNKS
    copies = []
    for b in range(OUT_CHUNKS):
        at = pl.ds(b * rows, rows)
        scale = spread(inv_ref[at, :], feats)
        unit = student_ref[at, :].astype(jnp.float32) * scale
        grad = scale * (4.0 * pull_ref[at, :])
        grad = grad - scale * unit * spread(4.0 * along_ref[at, :], feats)
        buf[at, :] = grad.astype(buf.dtype)
        copy = pltpu.make_async_copy(buf.at[at], out_hbm.at[0, at], sem.at[b])
        copy.start()
        copies.append(copy)
    total_ref[...] = loss_ref[0:1, 0:1]
    for copy in copies:
        copy.wait()


def per_device(n, m, student, teacher):
    _, tokens, feats = student.shape
    _, height, width, _ = teacher.shape
    nb = tokens // BLOCK
    _, first, quick = plan(nb)
    count = first[-1]
    tiles = tokens // LANES
    f32, bf16 = jnp.float32, jnp.bfloat16
    vmem, dma = pltpu.VMEM, pltpu.SemaphoreType.DMA
    features, pull, inv, along, loss = pl.pallas_call(
        functools.partial(kernel, (n, m)),
        name="anchor",
        out_shape=(
            jax.ShapeDtypeStruct((tokens, feats), bf16),
            jax.ShapeDtypeStruct((tokens, feats), f32),
            jax.ShapeDtypeStruct((tokens, LANES), f32),
            jax.ShapeDtypeStruct((tokens, LANES), f32),
            jax.ShapeDtypeStruct((8, LANES), f32),
        ),
        in_specs=[
            pl.BlockSpec(memory_space=pltpu.HBM),
            pl.BlockSpec(memory_space=pltpu.HBM),
        ],
        out_specs=(pl.BlockSpec(memory_space=pltpu.VMEM),) * 5,
        scratch_shapes=[
            vmem((height + 2, width, feats), bf16),
            vmem((UNROLL, feats // LANES, width + 16, LANES), f32),
            vmem((tokens, feats), f32),
            vmem((tokens, feats), bf16),
            vmem((tokens, feats), bf16),
            vmem((tokens, LANES), f32),
            vmem((tokens, LANES), f32),
            vmem((GROUPS, n, 2 * tiles // GROUPS, LANES), f32),
            vmem((n, tiles, LANES), f32),
            vmem((n, tiles + 8, LANES), f32),
            vmem((m, 8, LANES), f32),
            vmem((2, count, PIECE, BLOCK), f32),
            vmem((count, PIECE, BLOCK), f32),
            vmem((count, PIECE, BLOCK), bf16),
            vmem((count, PIECE, BLOCK), bf16),
            vmem((2, quick, HALF, BLOCK), bf16),
            vmem((2, quick, HALF, BLOCK), bf16),
            vmem((GROUPS, 2 * tiles // GROUPS, LANES), f32),
            vmem((2, count, PIECE, BLOCK), bf16),
            vmem((2, count, PIECE, BLOCK), bf16),
            vmem((2, count, PIECE, BLOCK), bf16),
            vmem((1, BLOCK), f32),
            dma((2 * CHUNKS + 2,)),
            dma((GROUPS, n - 1)), dma((GROUPS, n - 1)), dma((n - 1,)), dma((n - 1,)),
            dma((n - 1,)), dma((n - 1,)),
            dma((m - 1,)), dma((m - 1,)),
            dma((count,)), dma((count,)),
            dma((2, quick)), dma((2, quick)),
            dma((2, count)), dma((2, count)),
            dma((count,)), dma((count,)),
        ],
        compiler_params=pltpu.CompilerParams(
            collective_id=0, has_side_effects=True, vmem_limit_bytes=32 * 1024 * 1024
        ),
    )(*(pltpu.with_memory_space_constraint(x, pltpu.HBM) for x in (student, teacher)))
    gradient, total = pl.pallas_call(
        finish,
        name="finish",
        out_shape=(
            jax.ShapeDtypeStruct(student.shape, bf16),
            jax.ShapeDtypeStruct((1, 1), f32),
        ),
        in_specs=[pl.BlockSpec(memory_space=pltpu.VMEM)] * 5,
        out_specs=(
            pl.BlockSpec(memory_space=pl.ANY),
            pl.BlockSpec(memory_space=pltpu.VMEM),
        ),
        scratch_shapes=[vmem((tokens, feats), bf16), dma((OUT_CHUNKS,))],
        compiler_params=pltpu.CompilerParams(vmem_limit_bytes=16 * 1024 * 1024),
    )(features, pull, inv, along, loss)
    return gradient, total.reshape(())


def solution(mesh):
    return jax.shard_map(
        functools.partial(per_device, mesh.shape["tok"], mesh.shape["img"]),
        mesh=mesh,
        in_specs=(P("img", None, "tok"), P("img", None, None, "tok")),
        out_specs=(P("img", None, "tok"), P()),
        check_vma=False,
    )
```
